256 devices in a mesh: dp: 32 (over x, z), ctx: 8 (over y, core).
Axes of the slice: x: 4, y: 4, z: 8, core: 2. Of those that a mesh axis runs over, the one named last changes fastest.
Arguments:
- hidden: bfloat16 [32, 2048, 4096], P('dp', 'ctx'), may hold values from -6 to 6
- segments: int32 [32, 2048], P('dp', 'ctx'), may hold values from 0 to 15, as said below
- gain: float32 [4096], replicated, may hold values from 0.25 to 1.75
- inv_temp: float32 [], replicated, may hold values from 20 to 50
- positives: int32 [512], P(('dp', 'ctx')), may hold values from 0 to 511, as said below
Outputs:
- grad_hidden: bfloat16 [32, 2048, 4096], P('dp', 'ctx')
- grad_gain: float32 [4096], replicated
- loss: float32 [], replicated
The draws below stay inside these ranges and needn't reach their ends.
Inputs may be any that keep to these rules, and one draw needn't show every extreme that they name: `segments`: in each sequence the document numbers never fall along positions and every document has one position or more; document 0 covers more than half of the sequence's positions. `positives`: no document is its own positive.
All inputs are finite; a program needn't handle non-finite values.
Results may differ from the reference program's by a relative error of at most 0.0053.
Values may be sent and summed in bfloat16 or wider, within the bound.
A program may use at most 64 MiB of HBM per device.

```python
import jax
import jax.numpy as jnp
from jax import lax

D = 4096
TOKENS_PER_SHARD = 256
SEQ = 2048
DOCS_SEQ = 16
ALL_DOCS = 512
N_DP = 32


def one_sequence(key):
    first_len = SEQ // 2 + 1 + jax.random.randint(jax.random.fold_in(key, 1), (), 0, TOKENS_PER_SHARD).astype(jnp.int32)
    rest = SEQ - first_len
    spots = jnp.arange(SEQ, dtype=jnp.int32)
    scores = jax.random.randint(jax.random.fold_in(key, 2), (SEQ,), 0, SEQ).astype(jnp.int32) * SEQ + spots
    valid = jnp.logical_and(spots >= 1, spots <= rest - 1)
    scores = jnp.where(valid, scores, -1)
    picked = lax.top_k(scores, DOCS_SEQ - 2)[1].astype(jnp.int32)
    offset = spots - first_len
    after_first = (spots >= first_len).astype(jnp.int32)
    crossed = jnp.sum((offset[:, None] >= picked[None, :]).astype(jnp.int32), axis=1).astype(jnp.int32)
    return (after_first + after_first * crossed).astype(jnp.int32)


def draw_segments(key, part):
    keys = jax.random.split(jax.random.fold_in(key, 11), N_DP)
    return jax.vmap(one_sequence)(keys).astype(jnp.int32)


def draw_positives(key, part):
    order = jax.random.permutation(jax.random.fold_in(key, 7), ALL_DOCS).astype(jnp.int32)
    series = jnp.arange(ALL_DOCS, dtype=jnp.int32)
    return jnp.where(order == series, (series + 1) % ALL_DOCS, order).astype(jnp.int32)


def steps_of(stream_key, shape, cuts, smallest, largest):
    def one(axis_at, parts):
        heights = jax.random.uniform(jax.random.fold_in(jax.random.fold_in(stream_key, 6), axis_at), (parts,), jnp.float32, smallest / len(cuts), largest / len(cuts))
        return jnp.repeat(jnp.exp(heights), shape[axis_at] // parts).reshape((-1,) + (1,) * (len(shape) - axis_at - 1))

    level = one(*cuts[0])
    for cut in cuts[1:]:
        level = level * one(*cut)
    return level


def normal_values(own_key, dims, width, bound, shards=(), kind=jnp.bfloat16):
    drawn = jax.random.normal(own_key, dims, jnp.float32) * width
    if len(shards) > 0:
        drawn = steps_of(own_key, dims, shards, -0.22, 0.18) * drawn
    return jnp.clip(drawn, min=-bound, max=bound).astype(kind)


def setup_inputs(seed: int = 0) -> dict:
    key_of = jax.random.split(jax.random.key(seed), 6)
    return {
        "hidden": normal_values(key_of[0], (N_DP, SEQ, D), 1.0, 6.0, ((0, 32), (1, 8))),
        "segments": draw_segments(jax.random.fold_in(key_of[5], 71), 0),
        "gain": jnp.clip(1.0 + 0.15 * jax.random.normal(key_of[2], (D,), jnp.float32), 0.25, 1.75),
        "inv_temp": jnp.clip(jax.random.uniform(key_of[3], (), jnp.float32, 20.0, 50.0), 20.0, 50.0),
        "positives": draw_positives(jax.random.fold_in(key_of[5], 71), 0),
    }


def reference(hidden, segments, gain, inv_temp, positives):
    states = hidden.astype(jnp.float32)
    scale_t = lax.rsqrt(lax.optimization_barrier(jnp.mean(states * states, axis=-1, keepdims=True)) + 1e-06)
    normalized_rows = states * scale_t * gain
    document_indicator = (segments[:, :, None] == jnp.arange(DOCS_SEQ, dtype=jnp.int32)[None, None, :]).astype(jnp.float32)
    pooled_totals = jnp.einsum('eux,euj->exj', document_indicator, normalized_rows, precision=lax.Precision.HIGHEST)
    counts = lax.optimization_barrier(jnp.sum(document_indicator, axis=1))
    pooled = (pooled_totals / counts[:, :, None]).reshape(ALL_DOCS, D)
    rnorm = lax.rsqrt(lax.optimization_barrier(jnp.sum(pooled * pooled, axis=-1, keepdims=True)) + 1e-06)
    emb_f = pooled * rnorm
    emb = emb_f.astype(jnp.bfloat16)
    logits = jnp.dot(emb, emb.T, preferred_element_type=jnp.float32) * inv_temp
    rows = jnp.arange(ALL_DOCS, dtype=jnp.int32)
    self_mask = rows[:, None] == rows[None, :]
    pos_mask = (rows[None, :] == positives[:, None]).astype(jnp.float32)
    logits = jnp.where(self_mask, -1e+30, logits)
    top = lax.optimization_barrier(jnp.max(logits, axis=1, keepdims=True))
    expo = jnp.exp(logits - top)
    total = lax.optimization_barrier(jnp.sum(expo, axis=1, keepdims=True))
    lse = top[:, 0] + jnp.log(total[:, 0])
    pos_logit = lax.optimization_barrier(jnp.sum(pos_mask * logits, axis=1))
    loss = jnp.sum(lse - pos_logit) / ALL_DOCS
    gmat = ((expo / total - pos_mask) * (inv_temp / ALL_DOCS)).astype(jnp.bfloat16)
    demb = jnp.dot(gmat, emb, preferred_element_type=jnp.float32) + jnp.dot(gmat.T, emb, preferred_element_type=jnp.float32)
    dpool = rnorm * (demb - emb_f * lax.optimization_barrier(jnp.sum(emb_f * demb, axis=-1, keepdims=True)))
    sum_gradient = dpool.reshape(N_DP, DOCS_SEQ, D) / counts[:, :, None]
    normalized_gradient = jnp.einsum('gfa,gao->gfo', document_indicator, sum_gradient, precision=lax.Precision.HIGHEST)
    grad_gain = lax.optimization_barrier(jnp.sum(normalized_gradient * states * scale_t, axis=(0, 1)))
    grad_out = normalized_gradient * gain
    inner = lax.optimization_barrier(jnp.mean(grad_out * states, axis=-1, keepdims=True))
    grad_hidden = (scale_t * grad_out - states * scale_t ** 3 * inner).astype(jnp.bfloat16)
    return (grad_hidden, grad_gain, loss)
```

```python
import functools

import jax
import jax.numpy as jnp
from jax import lax
from jax.experimental import pallas as pl
from jax.experimental.pallas import tpu as pltpu
from jax.sharding import PartitionSpec as P

MESH = pl.DeviceIdType.MESH
F32 = jnp.float32
BF16 = jnp.bfloat16

NX, NY, NZ = 4, 4, 8
N_DP, N_CTX = NX * NZ, NY * 2
DOCS = 16
ALL = N_DP * DOCS
TOK = 256
D = 4096
FB = D // N_CTX
PAIR_ORDER = (0, 1, 3, 2)
RB = 128


def mod(a, n):
    return lax.rem(a, n)


def dot(a, b, dims):
    return lax.dot_general(a, b, (dims, ((), ())), preferred_element_type=F32)


def gather_kernel(
    h_hbm, seg_ref, pos_ref, gain_ref, it_ref,
    gd_ref, oh_ref, sc_ref, gg_ref, loss_ref,
    h, part, recv, emb, meta_own, meta_ctx, meta, gram, nmat, tbuf,
    h_sem, m1_send, m1_recv, mz_send, mz_recv, mx_send, mx_recv, p1_send, p1_recv,
    z_send, z_recv, a_send, a_recv, b_send, b_recv, s_send, s_recv,
):
    dp, ctx = lax.axis_index("dp"), lax.axis_index("ctx")
    x, z = lax.div(dp, NZ), mod(dp, NZ)
    y, c = lax.div(ctx, 2), mod(ctx, 2)
    a = (1 - c) * x + c * y
    b = (1 - c) * y + c * x

    def at_a(aa):
        return ((1 - c) * (aa * NZ + z) + c * dp, (1 - c) * ctx + c * (aa * 2 + c))

    def at_b(bb):
        return ((1 - c) * dp + c * (bb * NZ + z), (1 - c) * (bb * 2 + c) + c * ctx)

    sibling = (dp, ctx + 1 - 2 * c)

    barrier = pltpu.get_barrier_semaphore()
    peers = [(dp, mod(ctx + k, N_CTX)) for k in range(1, N_CTX)]
    peers += [(x * NZ + mod(z + k, NZ), ctx) for k in range(1, NZ)]
    peers += [(mod(x + k, NX) * NZ + z, ctx) for k in range(1, NX)]
    for peer in peers:
        pl.semaphore_signal(barrier, inc=1, device_id=peer, device_id_type=MESH)

    h_copies = []
    for i in range(4):
        rows = pl.ds(i * (TOK // 4), TOK // 4)
        h_copies.append(pltpu.make_async_copy(h_hbm.at[rows], h.at[rows], h_sem.at[i]))
        h_copies[-1].start()

    seg = seg_ref[...]
    doc_rows = lax.broadcasted_iota(jnp.int32, (DOCS, TOK), 0)
    onehot = (seg == doc_rows).astype(F32)
    doc_col = lax.broadcasted_iota(jnp.int32, (DOCS, 128), 0)
    lane = lax.broadcasted_iota(jnp.int32, (DOCS, 128), 1)
    pos = jnp.where(doc_col == 2 * ctx, pos_ref[0], jnp.where(doc_col == 2 * ctx + 1, pos_ref[1], 0))
    meta_own[...] = jnp.where(lane == 0, pos.astype(F32), jnp.sum(onehot, axis=1, keepdims=True))

    squares = []
    for i in range(4):
        h_copies[i].wait()
        acc = jnp.zeros((TOK // 4, 128), F32)
        for j in range(D // 128):
            v = h[i * (TOK // 4):(i + 1) * (TOK // 4), j * 128:(j + 1) * 128].astype(F32)
            acc = acc + v * v
        squares.append(jnp.sum(acc, axis=1, keepdims=True))
    mean_sq = jnp.concatenate(squares, axis=0) * (1.0 / D)
    scale = jnp.broadcast_to(lax.rsqrt(mean_sq + 1e-06), (TOK, 128))
    sc_ref[...] = scale
    weight = onehot * jnp.transpose(scale)[0:DOCS, :]
    w_hi = weight.astype(BF16)
    w_lo = (weight - w_hi.astype(F32)).astype(BF16)
    w2 = jnp.concatenate([w_hi, w_lo], axis=0)
    for j in range(N_CTX):
        cols = slice(j * FB, (j + 1) * FB)
        both = dot(w2, h[:, cols], ((1,), (0,)))
        part[:, cols] = ((both[0:DOCS] + both[DOCS:]) * gain_ref[:, cols]).astype(BF16)

    pl.semaphore_wait(barrier, len(peers))

    def p1(src, dst):
        return pltpu.make_async_remote_copy(
            src_ref=part.at[:, pl.ds(pl.multiple_of(dst * FB, FB), FB)], dst_ref=recv.at[src],
            send_sem=p1_send, recv_sem=p1_recv.at[src], device_id=(dp, dst), device_id_type=MESH,
        )

    def m1(src, dst):
        return pltpu.make_async_remote_copy(
            src_ref=meta_own, dst_ref=meta_ctx.at[src],
            send_sem=m1_send, recv_sem=m1_recv.at[src], device_id=(dp, dst), device_id_type=MESH,
        )

    others = [mod(ctx + k, N_CTX) for k in (4, 5, 3, 2, 6, 7, 1)]
    for other in others:
        p1(ctx, other).start()
    for other in others:
        m1(ctx, other).start()

    my_col = pl.ds(pl.multiple_of(ctx * FB, FB), FB)
    total = part[:, my_col].astype(F32)
    for other in reversed(others):
        p1(other, ctx).wait_recv()
        total = total + recv[other].astype(F32)
    emb[dp, :, my_col] = total.astype(BF16)

    def zcopy(zz, dst):
        ref = emb.at[x * NZ + zz, :, my_col]
        return pltpu.make_async_remote_copy(
            src_ref=ref, dst_ref=ref, send_sem=z_send, recv_sem=z_recv.at[zz],
            device_id=(x * NZ + dst, ctx), device_id_type=MESH,
        )

    for k in (4, 3, 5, 2, 6, 1, 7):
        zcopy(z, mod(z + k, NZ)).start()

    def mz(zz, dst):
        ref = meta.at[x * NZ + zz]
        return pltpu.make_async_remote_copy(
            src_ref=ref, dst_ref=ref, send_sem=mz_send, recv_sem=mz_recv.at[zz],
            device_id=(x * NZ + dst, ctx), device_id_type=MESH,
        )

    def mx(xx, dst):
        ref = meta.at[pl.ds(xx * NZ, NZ)]
        return pltpu.make_async_remote_copy(
            src_ref=ref, dst_ref=ref, send_sem=mx_send, recv_sem=mx_recv.at[xx],
            device_id=(dst * NZ + z, ctx), device_id_type=MESH,
        )

    meta_sum = meta_own[...]
    for other in others:
        m1(other, ctx).wait_recv()
        meta_sum = meta_sum + meta_ctx[other]
    meta[dp] = meta_sum
    for k in range(1, NZ):
        mz(z, mod(z + k, NZ)).start()

    a_off = lambda k: mod(a + k, NX)
    b_off = lambda k: mod(b + k, NX)
    pair_of = lambda k: mod(lax.div(z, 2) + PAIR_ORDER[k], NZ // 2)

    def block(aa, bb, k):
        xx = (1 - c) * aa + c * bb
        yy = (1 - c) * bb + c * aa
        col = pl.multiple_of((yy * 2 + c) * FB, FB)
        return emb.at[pl.ds(xx * NZ + 2 * pair_of(k), 2), :, pl.ds(col, FB)]

    def acopy(aa, k, way, to):
        ref = block(aa, b, k)
        return pltpu.make_async_remote_copy(
            src_ref=ref, dst_ref=ref, send_sem=a_send, recv_sem=a_recv.at[3 * k + way],
            device_id=at_a(to), device_id_type=MESH,
        )

    def bcopy(am, bb, k, way, to):
        ref = block(a_off(am), bb, k)
        return pltpu.make_async_remote_copy(
            src_ref=ref, dst_ref=ref, send_sem=b_send, recv_sem=b_recv.at[12 * k + 3 * am + way],
            device_id=at_b(to), device_id_type=MESH,
        )

    def sib(am, bm, k):
        ref = block(a_off(am), b_off(bm), k)
        return pltpu.make_async_remote_copy(
            src_ref=ref, dst_ref=ref, send_sem=s_send, recv_sem=s_recv,
            device_id=sibling, device_id_type=MESH,
        )

    def a_start(k):
        acopy(a, k, 0, a_off(1)).start()
        acopy(a, k, 1, a_off(3)).start()

    def b_start(am, k):
        bcopy(am, b, k, 0, b_off(1)).start()
        bcopy(am, b, k, 1, b_off(3)).start()
        sib(am, 0, k).start()

    def a_relay(k):
        acopy(a_off(3), k, 0, a).wait_recv()
        acopy(a_off(1), k, 1, a).wait_recv()
        if k % 2 == 0:
            acopy(a_off(3), k, 2, a_off(1)).start()
        else:
            acopy(a_off(1), k, 2, a_off(3)).start()
        b_start(3, k)
        b_start(1, k)

    def a_last(k):
        acopy(a_off(2), k, 2, a).wait_recv()
        b_start(2, k)

    def b_relay(am, k):
        bcopy(am, b_off(3), k, 0, b).wait_recv()
        bcopy(am, b_off(1), k, 1, b).wait_recv()
        if (k + (am == 2)) % 2 == 0:
            bcopy(am, b_off(3), k, 2, b_off(1)).start()
        else:
            bcopy(am, b_off(1), k, 2, b_off(3)).start()
        sib(am, 3, k).start()
        sib(am, 1, k).start()

    def b_last(am, k):
        bcopy(am, b_off(2), k, 2, b).wait_recv()
        sib(am, 2, k).start()

    for t in range(9):
        if t < 4:
            for i in range(2):
                zz = 2 * pair_of(t) + i
                if t == 0:
                    zz = z + 1 - 2 * mod(z, 2)
                    if i == 1:
                        continue
                zcopy(zz, z).wait_recv()
            a_start(t)
            b_start(0, t)
        if 1 <= t < 5:
            a_relay(t - 1)
            b_relay(0, t - 1)
        if 2 <= t < 6:
            a_last(t - 2)
            b_relay(3, t - 2)
            b_relay(1, t - 2)
            b_last(0, t - 2)
        if 3 <= t < 7:
            b_relay(2, t - 3)
            b_last(3, t - 3)
            b_last(1, t - 3)
        if 4 <= t < 8:
            b_last(2, t - 4)
        if t == 3:
            for k in range(1, NZ):
                mz(mod(z + k, NZ), z).wait_recv()
            for k in range(1, NX):
                mx(x, mod(x + k, NX)).start()

    gram[...] = jnp.zeros_like(gram)

    def gram_of(core):
        @pl.loop(0, NY)
        def _(yy):
            col = pl.multiple_of((yy * 2 + core) * FB, FB)
            e = emb[:, :, pl.ds(col, FB)].reshape(ALL, FB)
            gram[...] += dot(e, e, ((1,), (1,)))

    gram_of(c)
    pltpu.make_async_remote_copy(
        src_ref=emb.at[pl.ds(0, N_DP // 2)], dst_ref=emb.at[pl.ds(0, N_DP // 2)],
        send_sem=s_send, recv_sem=s_recv, device_id=sibling, device_id_type=MESH,
    ).wait_recv()
    gram_of(1 - c)

    for k in range(1, NX):
        mx(mod(x + k, NX), x).wait_recv()

    inv_temp = it_ref[0]
    info = meta[...].reshape(ALL, 128)
    pos_col, count_col = info[:, 0:1].astype(jnp.int32), info[:, 1:2]
    eye = lax.broadcasted_iota(jnp.int32, (RB, RB), 0) == lax.broadcasted_iota(jnp.int32, (RB, RB), 1)
    blocks = [slice(i * RB, (i + 1) * RB) for i in range(ALL // RB)]

    def as_row(cols):
        return jnp.concatenate(
            [jnp.sum(jnp.where(eye, jnp.broadcast_to(v, (RB, RB)), 0.0), axis=0, keepdims=True) for v in cols],
            axis=1,
        )

    q_cols = []
    for r in blocks:
        norm2 = jnp.sum(jnp.where(eye, gram[r, r], 0.0), axis=1, keepdims=True)
        inv_count = 1.0 / count_col[r]
        q_cols.append(inv_count * lax.rsqrt(norm2 * inv_count * inv_count + 1e-06))
    q_row = as_row(q_cols)
    pos_row = as_row([info[r, 0:1] for r in blocks]).astype(jnp.int32)

    lane_all = lax.broadcasted_iota(jnp.int32, (RB, ALL), 1)
    sub_all = lax.broadcasted_iota(jnp.int32, (RB, ALL), 0)
    lse_cols = []
    loss = jnp.zeros((1, 1), F32)
    for i, r in enumerate(blocks):
        cosine = gram[r, :] * q_cols[i] * q_row
        gram[r, :] = cosine
        logits = jnp.where(lane_all == sub_all + i * RB, -1e30, cosine * inv_temp)
        top = jnp.max(logits, axis=1, keepdims=True)
        sum_exp = jnp.sum(jnp.exp(logits - top), axis=1, keepdims=True)
        lse = top + jnp.log(sum_exp)
        at_pos = jnp.sum(jnp.where(lane_all == pos_col[r], logits, 0.0), axis=1, keepdims=True)
        loss = loss + jnp.sum(lse - at_pos, axis=0, keepdims=True)
        lse_cols.append(lse)
    loss_ref[...] = jnp.broadcast_to(loss * (1.0 / ALL), (1, 128))
    lse_row = as_row(lse_cols)

    for i, r in enumerate(blocks):
        cosine = gram[r, :]
        diagonal = lane_all == sub_all + i * RB
        logits = jnp.where(diagonal, -1e30, cosine * inv_temp)
        own = jnp.exp(logits - lse_cols[i]) - (lane_all == pos_col[r]).astype(F32)
        other = jnp.exp(logits - lse_row) - (sub_all + i * RB == pos_row).astype(F32)
        both = (own + other) * (inv_temp * (1.0 / ALL))
        along = jnp.sum(both * cosine, axis=1, keepdims=True)
        nmat[r, :] = ((both - jnp.where(diagonal, along, 0.0)) * q_cols[i] * q_row).astype(BF16)

    n_all = nmat[...]
    my_rows = pl.ds(pl.multiple_of(dp * DOCS, DOCS), DOCS)

    @pl.loop(0, N_CTX)
    def _(j):
        cols = pl.ds(pl.multiple_of(j * FB, FB), FB)
        e = emb[:, :, cols].reshape(ALL, FB)
        tbuf[...] = dot(n_all, e, ((1,), (0,)))
        gain = gain_ref[:, cols]
        gg_ref[:, cols] = jnp.sum(tbuf[...] * e.astype(F32), axis=0, keepdims=True) / gain
        g16 = tbuf[my_rows, :] * gain
        g_hi = g16.astype(BF16)
        gd_ref[0:DOCS, cols] = g_hi
        gd_ref[DOCS:, cols] = (g16 - g_hi.astype(F32)).astype(BF16)

    oh = jnp.concatenate([onehot, onehot, jnp.zeros((128 - 2 * DOCS, TOK), F32)], axis=0)
    oh_ref[...] = jnp.transpose(oh).astype(BF16)

    def sent(ref, sem):
        pltpu.make_async_remote_copy(
            src_ref=ref, dst_ref=ref, send_sem=sem, recv_sem=s_recv, device_id=sibling, device_id_type=MESH,
        ).wait_send()

    sent(recv.at[pl.ds(0, N_CTX - 1)], p1_send)
    sent(meta_ctx.at[pl.ds(0, N_CTX - 1)], m1_send)
    sent(emb.at[pl.ds(0, NZ - 1), :, pl.ds(0, FB)], z_send)
    sent(meta.at[pl.ds(0, NZ - 1)], mz_send)
    sent(meta.at[pl.ds(0, NZ * (NX - 1))], mx_send)
    sent(emb.at[pl.ds(0, 3)], a_send)
    sent(emb.at[pl.ds(0, 12)], b_send)
    sent(emb.at[pl.ds(0, 16)], s_send)


def final_kernel(h_ref, gd_ref, oh_ref, sc_ref, gg_ref, loss_ref, out_ref, gg_out, loss_out):
    states = h_ref[0]
    gd2 = gd_ref[...]
    select = oh_ref[:, 0:2 * DOCS]
    scale = sc_ref[:, 0:1]
    inner = dot(states, gd2, ((1,), (1,))) * select.astype(F32)
    inner = jnp.sum(inner, axis=1, keepdims=True) * (1.0 / D)
    coef = scale * scale * scale * inner
    for j in range(D // 512):
        cols = slice(j * 512, (j + 1) * 512)
        grad = dot(select, gd2[:, cols], ((1,), (0,)))
        out_ref[0, :, cols] = (scale * grad - states[:, cols].astype(F32) * coef).astype(BF16)
    gg_out[...] = gg_ref[...]
    loss_out[...] = loss_ref[...]


def body(hidden, segments, gain, inv_temp, positives):
    vmem = pl.BlockSpec(memory_space=pltpu.VMEM)
    smem = pl.BlockSpec(memory_space=pltpu.SMEM)
    dma = pltpu.SemaphoreType.DMA
    gd, oh, sc, gg, loss = pl.pallas_call(
        gather_kernel,
        name="pool_gather",
        out_shape=(
            jax.ShapeDtypeStruct((2 * DOCS, D), BF16),
            jax.ShapeDtypeStruct((TOK, 128), BF16),
            jax.ShapeDtypeStruct((TOK, 128), F32),
            jax.ShapeDtypeStruct((1, D), F32),
            jax.ShapeDtypeStruct((1, 128), F32),
        ),
        in_specs=[pl.BlockSpec(memory_space=pl.ANY), vmem, smem, vmem, smem],
        out_specs=(vmem,) * 5,
        scratch_shapes=[
            pltpu.VMEM((TOK, D), BF16),
            pltpu.VMEM((DOCS, D), BF16),
            pltpu.VMEM((N_CTX, DOCS, FB), BF16),
            pltpu.VMEM((N_DP, DOCS, D), BF16),
            pltpu.VMEM((DOCS, 128), F32),
            pltpu.VMEM((N_CTX, DOCS, 128), F32),
            pltpu.VMEM((N_DP, DOCS, 128), F32),
            pltpu.VMEM((ALL, ALL), F32),
            pltpu.VMEM((ALL, ALL), BF16),
            pltpu.VMEM((ALL, FB), F32),
            dma((4,)),
            dma, dma((N_CTX,)), dma, dma((NZ,)), dma, dma((NX,)), dma, dma((N_CTX,)),
            dma, dma((NZ,)), dma, dma((12,)), dma, dma((48,)), dma, dma,
        ],
        compiler_params=pltpu.CompilerParams(collective_id=0, has_side_effects=True),
    )(hidden[0], segments, positives, gain.reshape(1, D), inv_temp.reshape(1))

    rows = 64
    whole = lambda shape: pl.BlockSpec(shape, lambda i: (0, 0))
    grad_hidden, grad_gain, loss = pl.pallas_call(
        final_kernel,
        name="grad_hidden",
        grid=(TOK // rows,),
        out_shape=(
            jax.ShapeDtypeStruct((1, TOK, D), BF16),
            jax.ShapeDtypeStruct((1, D), F32),
            jax.ShapeDtypeStruct((1, 128), F32),
        ),
        in_specs=[
            pl.BlockSpec((1, rows, D), lambda i: (0, i, 0)),
            whole((2 * DOCS, D)),
            pl.BlockSpec((rows, 128), lambda i: (i, 0)),
            pl.BlockSpec((rows, 128), lambda i: (i, 0)),
            whole((1, D)),
            whole((1, 128)),
        ],
        out_specs=(pl.BlockSpec((1, rows, D), lambda i: (0, i, 0)), whole((1, D)), whole((1, 128))),
    )(hidden, gd, oh, sc, gg, loss)
    return grad_hidden, grad_gain.reshape(D), loss[0, 0]


def solution(mesh):
    return jax.shard_map(
        body,
        mesh=mesh,
        in_specs=(P("dp", "ctx", None), P("dp", "ctx"), P(), P(), P(("dp", "ctx"))),
        out_specs=(P("dp", "ctx", None), P(), P()),
        check_vma=False,
    )
```

```python
import functools

import jax
import jax.numpy as jnp
from jax import lax
from jax.experimental import pallas as pl
from jax.experimental.pallas import tpu as pltpu
from jax.sharding import PartitionSpec as P

MESH = pl.DeviceIdType.MESH
F32 = jnp.float32
BF16 = jnp.bfloat16

NX, NY, NZ = 4, 4, 8
N_DP, N_CTX = NX * NZ, NY * 2
DOCS = 16
ALL = N_DP * DOCS
TOK = 256
D = 4096
FB = D // N_CTX
RB = 128


def mod(a, n):
    return lax.rem(a, n)


def dot(a, b, dims):
    return lax.dot_general(a, b, (dims, ((), ())), preferred_element_type=F32)


def gather_kernel(
    h_hbm, seg_ref, pos_ref, gain_ref, it_ref,
    gd_ref, oh_ref, sc_ref, gg_ref, loss_ref,
    h, part, recv, emb, meta_own, meta_ctx, meta, gram, nmat, tbuf,
    h_sem, m1_send, m1_recv, mz_send, mz_recv, mx_send, mx_recv, p1_send, p1_recv,
    z_send, z_recv, a_send, a_recv, b_send, b_recv, s_send, s_recv,
):
    dp, ctx = lax.axis_index("dp"), lax.axis_index("ctx")
    x, z = lax.div(dp, NZ), mod(dp, NZ)
    y, c = lax.div(ctx, 2), mod(ctx, 2)
    a = (1 - c) * x + c * y
    b = (1 - c) * y + c * x

    h_copies = []
    for i in range(4):
        rows = pl.ds(i * (TOK // 4), TOK // 4)
        h_copies.append(pltpu.make_async_copy(h_hbm.at[rows], h.at[rows], h_sem.at[i]))
        h_copies[-1].start()

    def at_a(aa):
        return ((1 - c) * (aa * NZ + z) + c * dp, (1 - c) * ctx + c * (aa * 2 + c))

    def at_b(bb):
        return ((1 - c) * dp + c * (bb * NZ + z), (1 - c) * (bb * 2 + c) + c * ctx)

    sibling = (dp, ctx + 1 - 2 * c)

    barrier = pltpu.get_barrier_semaphore()
    peers = [(x * NZ + mod(z + k, NZ), ctx) for k in (4, 3, 5, 2, 6, 1, 7)]
    peers += [(dp, mod(ctx + k, N_CTX)) for k in range(1, N_CTX)]
    peers += [(mod(x + k, NX) * NZ + z, ctx) for k in range(1, NX)]
    for peer in peers:
        pl.semaphore_signal(barrier, inc=1, device_id=peer, device_id_type=MESH)

    seg = seg_ref[...]
    doc_rows = lax.broadcasted_iota(jnp.int32, (DOCS, TOK), 0)
    onehot = (seg == doc_rows).astype(F32)
    lane = lax.broadcasted_iota(jnp.int32, (DOCS, 128), 1)
    counts = jnp.where(
        lane == DOCS + lax.broadcasted_iota(jnp.int32, (DOCS, 128), 0), jnp.sum(onehot, axis=1, keepdims=True), 0.0
    )
    lane1 = lax.broadcasted_iota(jnp.int32, (1, 128), 1)
    pos = jnp.where(lane1 == 2 * ctx, pos_ref[0], jnp.where(lane1 == 2 * ctx + 1, pos_ref[1], 0))
    meta_own[...] = pos.astype(F32) + jnp.sum(counts, axis=0, keepdims=True)

    squares = []
    for i in range(4):
        h_copies[i].wait()
        acc = jnp.zeros((TOK // 4, 128), F32)
        for j in range(D // 128):
            v = h[i * (TOK // 4):(i + 1) * (TOK // 4), j * 128:(j + 1) * 128].astype(F32)
            acc = acc + v * v
        squares.append(jnp.sum(acc, axis=1, keepdims=True))
    mean_sq = jnp.concatenate(squares, axis=0) * (1.0 / D)
    scale = jnp.broadcast_to(lax.rsqrt(mean_sq + 1e-06), (TOK, 128))
    sc_ref[...] = scale
    weight = onehot * jnp.transpose(scale)[0:DOCS, :]
    w_hi = weight.astype(BF16)
    w_lo = (weight - w_hi.astype(F32)).astype(BF16)
    w2 = jnp.concatenate([w_hi, w_lo], axis=0)

    pl.semaphore_wait(barrier, len(peers))

    def p1(src, dst):
        return pltpu.make_async_remote_copy(
            src_ref=part.at[:, pl.ds(pl.multiple_of(dst * FB, FB), FB)], dst_ref=recv.at[src],
            send_sem=p1_send, recv_sem=p1_recv.at[src], device_id=(dp, dst), device_id_type=MESH,
        )

    def m1(src, dst):
        return pltpu.make_async_remote_copy(
            src_ref=meta_own, dst_ref=meta_ctx.at[src],
            send_sem=m1_send, recv_sem=m1_recv.at[src], device_id=(dp, dst), device_id_type=MESH,
        )

    def partial_sums(j):
        cols = pl.ds(pl.multiple_of(j * FB, FB), FB)
        both = dot(w2, h[:, cols], ((1,), (0,)))
        return (both[0:DOCS] + both[DOCS:]) * gain_ref[:, cols]

    others = [mod(ctx + k, N_CTX) for k in (4, 5, 3, 2, 6, 7, 1)]
    for other in others:
        m1(ctx, other).start()
    for other in others:
        part[:, pl.ds(pl.multiple_of(other * FB, FB), FB)] = partial_sums(other).astype(BF16)
        p1(ctx, other).start()

    my_col = pl.ds(pl.multiple_of(ctx * FB, FB), FB)
    total = partial_sums(ctx)
    for other in reversed(others):
        p1(other, ctx).wait_recv()
        total = total + recv[other].astype(F32)
    emb[dp, :, my_col] = total.astype(BF16)

    def zcopy(zz, dst):
        ref = emb.at[x * NZ + zz, :, my_col]
        return pltpu.make_async_remote_copy(
            src_ref=ref, dst_ref=ref, send_sem=z_send, recv_sem=z_recv.at[zz],
            device_id=(x * NZ + dst, ctx), device_id_type=MESH,
        )

    def mz(zz, dst):
        ref = meta.at[x * NZ + zz]
        return pltpu.make_async_remote_copy(
            src_ref=ref, dst_ref=ref, send_sem=mz_send, recv_sem=mz_recv.at[zz],
            device_id=(x * NZ + dst, ctx), device_id_type=MESH,
        )

    def mx(xx, dst):
        ref = meta.at[pl.ds(xx * NZ, NZ)]
        return pltpu.make_async_remote_copy(
            src_ref=ref, dst_ref=ref, send_sem=mx_send, recv_sem=mx_recv.at[xx],
            device_id=(dst * NZ + z, ctx), device_id_type=MESH,
        )

    partner = z + 1 - 2 * mod(z, 2)
    pair = lax.div(z, 2)
    pair_at = [2 * mod(pair + k, NZ // 2) for k in (1, 3, 2)]
    first = [z, partner] + pair_at
    size = [1, 1, 2, 2, 2]
    away = [partner] + [pair_at[i] + j for i in (1, 0, 2) for j in range(2)]

    a_off = lambda k: mod(a + k, NX)
    b_off = lambda k: mod(b + k, NX)

    def block(aa, bb, g):
        xx = (1 - c) * aa + c * bb
        yy = (1 - c) * bb + c * aa
        col = pl.multiple_of((yy * 2 + c) * FB, FB)
        return emb.at[pl.ds(xx * NZ + first[g], size[g]), :, pl.ds(col, FB)]

    def acopy(am, g, way, to):
        ref = block(a_off(am), b, g)
        return pltpu.make_async_remote_copy(
            src_ref=ref, dst_ref=ref, send_sem=a_send, recv_sem=a_recv.at[3 * g + way],
            device_id=at_a(to), device_id_type=MESH,
        )

    def bcopy(am, bm, g, way, to):
        ref = block(a_off(am), b_off(bm), g)
        return pltpu.make_async_remote_copy(
            src_ref=ref, dst_ref=ref, send_sem=b_send, recv_sem=b_recv.at[12 * g + 3 * am + way],
            device_id=at_b(to), device_id_type=MESH,
        )

    def sib(am, bm, g):
        ref = block(a_off(am), b_off(bm), g)
        pltpu.make_async_remote_copy(
            src_ref=ref, dst_ref=ref, send_sem=s_send, recv_sem=s_recv,
            device_id=sibling, device_id_type=MESH,
        ).start()

    def spread(am, g):
        bcopy(am, 0, g, 0, b_off(1)).start()
        bcopy(am, 0, g, 1, b_off(3)).start()
        sib(am, 0, g)

    def enter(g):
        for i in range(size[g]):
            if g > 0:
                zcopy(first[g] + i, z).wait_recv()
        for way, k in ((0, 1), (1, 3), (2, 2)):
            acopy(0, g, way, a_off(k)).start()
        spread(0, g)

    def along_a(g):
        for way, k in ((0, 3), (1, 1), (2, 2)):
            acopy(k, g, way, a).wait_recv()
            spread(k, g)

    def relay(am, g):
        bcopy(am, 3, g, 0, b).wait_recv()
        bcopy(am, 1, g, 1, b).wait_recv()
        if (g + (am >= 2)) % 2 == 0:
            bcopy(am, 3, g, 2, b_off(1)).start()
        else:
            bcopy(am, 1, g, 2, b_off(3)).start()
        sib(am, 3, g)
        sib(am, 1, g)

    def last(am, g):
        bcopy(am, 2, g, 2, b).wait_recv()
        sib(am, 2, g)

    for to in away:
        zcopy(z, to).start()
    enter(0)
    meta_sum = meta_own[...]
    for other in others:
        m1(other, ctx).wait_recv()
        meta_sum = meta_sum + meta_ctx[other]
    meta[dp] = meta_sum
    for to in away:
        mz(z, to).start()

    enter(1)
    along_a(0)
    enter(2)
    relay(0, 0)
    enter(3)
    along_a(1)
    relay(0, 1)
    enter(4)
    for am in (3, 1, 2):
        relay(am, 0)
    along_a(2)
    last(0, 0)
    for am in (3, 1, 2):
        relay(am, 1)
    relay(0, 2)
    along_a(3)
    for to in away:
        mz(to, z).wait_recv()
    for k in range(1, NX):
        mx(x, mod(x + k, NX)).start()
    for am in (3, 1, 2):
        last(am, 0)
    last(0, 1)
    relay(0, 3)
    along_a(4)
    for am in (3, 1, 2):
        relay(am, 2)
    relay(0, 4)
    for am in (3, 1, 2):
        last(am, 1)
    last(0, 2)
    for am in (3, 1, 2):
        relay(am, 3)
    last(0, 3)
    for am in (3, 1, 2):
        relay(am, 4)
    for am in (3, 1, 2):
        last(am, 2)
    for g in (3, 4):
        for am in (0, 3, 1, 2):
            if (am, g) != (0, 3):
                last(am, g)

    gram[...] = jnp.zeros_like(gram)

    def gram_of(core):
        @pl.loop(0, NY)
        def _(yy):
            col = pl.multiple_of((yy * 2 + core) * FB, FB)
            e = emb[:, :, pl.ds(col, FB)].reshape(ALL, FB)
            gram[...] += dot(e, e, ((1,), (1,)))

    gram_of(c)
    pltpu.make_async_remote_copy(
        src_ref=emb.at[pl.ds(0, N_DP // 2)], dst_ref=emb.at[pl.ds(0, N_DP // 2)],
        send_sem=s_send, recv_sem=s_recv, device_id=sibling, device_id_type=MESH,
    ).wait_recv()
    gram_of(1 - c)

    for k in range(1, NX):
        mx(mod(x + k, NX), x).wait_recv()

    inv_temp = it_ref[0]
    info = jnp.broadcast_to(meta[...], (N_DP, DOCS, 128)).reshape(ALL, 128)
    at = lax.broadcasted_iota(jnp.int32, (ALL, 128), 1) - mod(lax.broadcasted_iota(jnp.int32, (ALL, 128), 0), DOCS)
    pos_f = jnp.sum(jnp.where(at == 0, info, 0.0), axis=1, keepdims=True)
    pos_col = pos_f.astype(jnp.int32)
    count_col = jnp.sum(jnp.where(at == DOCS, info, 0.0), axis=1, keepdims=True)
    eye = lax.broadcasted_iota(jnp.int32, (RB, RB), 0) == lax.broadcasted_iota(jnp.int32, (RB, RB), 1)
    blocks = [slice(i * RB, (i + 1) * RB) for i in range(ALL // RB)]

    def as_row(cols):
        return jnp.concatenate(
            [jnp.sum(jnp.where(eye, jnp.broadcast_to(v, (RB, RB)), 0.0), axis=0, keepdims=True) for v in cols],
            axis=1,
        )

    q_cols = []
    for r in blocks:
        norm2 = jnp.sum(jnp.where(eye, gram[r, r], 0.0), axis=1, keepdims=True)
        inv_count = 1.0 / count_col[r]
        q_cols.append(inv_count * lax.rsqrt(norm2 * inv_count * inv_count + 1e-06))
    q_row = as_row(q_cols)
    pos_row = as_row([pos_f[r] for r in blocks]).astype(jnp.int32)

    lane_all = lax.broadcasted_iota(jnp.int32, (RB, ALL), 1)
    sub_all = lax.broadcasted_iota(jnp.int32, (RB, ALL), 0)
    lse_cols = []
    loss = jnp.zeros((1, 1), F32)
    for i, r in enumerate(blocks):
        cosine = gram[r, :] * q_cols[i] * q_row
        gram[r, :] = cosine
        logits = jnp.where(lane_all == sub_all + i * RB, -1e30, cosine * inv_temp)
        top = jnp.max(logits, axis=1, keepdims=True)
        sum_exp = jnp.sum(jnp.exp(logits - top), axis=1, keepdims=True)
        lse = top + jnp.log(sum_exp)
        at_pos = jnp.sum(jnp.where(lane_all == pos_col[r], logits, 0.0), axis=1, keepdims=True)
        loss = loss + jnp.sum(lse - at_pos, axis=0, keepdims=True)
        lse_cols.append(lse)
    loss_ref[...] = jnp.broadcast_to(loss * (1.0 / ALL), (1, 128))
    lse_row = as_row(lse_cols)

    for i, r in enumerate(blocks):
        cosine = gram[r, :]
        diagonal = lane_all == sub_all + i * RB
        logits = jnp.where(diagonal, -1e30, cosine * inv_temp)
        own = jnp.exp(logits - lse_cols[i]) - (lane_all == pos_col[r]).astype(F32)
        other = jnp.exp(logits - lse_row) - (sub_all + i * RB == pos_row).astype(F32)
        both = (own + other) * (inv_temp * (1.0 / ALL))
        along = jnp.sum(both * cosine, axis=1, keepdims=True)
        nmat[r, :] = ((both - jnp.where(diagonal, along, 0.0)) * q_cols[i] * q_row).astype(BF16)

    n_all = nmat[...]
    my_rows = pl.ds(pl.multiple_of(dp * DOCS, DOCS), DOCS)

    @pl.loop(0, N_CTX)
    def _(j):
        cols = pl.ds(pl.multiple_of(j * FB, FB), FB)
        e = emb[:, :, cols].reshape(ALL, FB)
        tbuf[...] = dot(n_all, e, ((1,), (0,)))
        gain = gain_ref[:, cols]
        gg_ref[:, cols] = jnp.sum(tbuf[...] * e.astype(F32), axis=0, keepdims=True) / gain
        g16 = tbuf[my_rows, :] * gain
        g_hi = g16.astype(BF16)
        gd_ref[0:DOCS, cols] = g_hi
        gd_ref[DOCS:, cols] = (g16 - g_hi.astype(F32)).astype(BF16)

    oh = jnp.concatenate([onehot, onehot, jnp.zeros((128 - 2 * DOCS, TOK), F32)], axis=0)
    oh_ref[...] = jnp.transpose(oh).astype(BF16)

    def sent(ref, sem):
        pltpu.make_async_remote_copy(
            src_ref=ref, dst_ref=ref, send_sem=sem, recv_sem=s_recv, device_id=sibling, device_id_type=MESH,
        ).wait_send()

    sent(recv.at[pl.ds(0, N_CTX - 1)], p1_send)
    sent(meta_ctx.at[pl.ds(0, N_CTX - 1)], m1_send)
    sent(emb.at[pl.ds(0, NZ - 1), :, pl.ds(0, FB)], z_send)
    sent(meta.at[pl.ds(0, NZ - 1)], mz_send)
    sent(meta.at[pl.ds(0, NZ * (NX - 1))], mx_send)
    sent(emb.at[pl.ds(0, 3)], a_send)
    sent(emb.at[pl.ds(0, 12)], b_send)
    sent(emb.at[pl.ds(0, 16)], s_send)


def final_kernel(h_ref, gd_ref, oh_ref, sc_ref, gg_ref, loss_ref, out_ref, gg_out, loss_out, grad):
    select = oh_ref[:, 0:2 * DOCS]
    scale = sc_ref[:, 0:1]
    acc = jnp.zeros((select.shape[0], 128), F32)
    for j in range(D // 512):
        cols = slice(j * 512, (j + 1) * 512)
        part = dot(select, gd_ref[:, cols], ((1,), (0,)))
        grad[:, cols] = part
        prod = part * h_ref[0, :, cols].astype(F32)
        for k in range(4):
            acc = acc + prod[:, k * 128:(k + 1) * 128]
    inner = jnp.sum(acc, axis=1, keepdims=True) * (1.0 / D)
    coef = scale * scale * scale * inner
    for j in range(D // 512):
        cols = slice(j * 512, (j + 1) * 512)
        out_ref[0, :, cols] = (scale * grad[:, cols] - h_ref[0, :, cols].astype(F32) * coef).astype(BF16)
    gg_out[...] = gg_ref[...]
    loss_out[...] = loss_ref[...]


def body(hidden, segments, gain, inv_temp, positives):
    vmem = pl.BlockSpec(memory_space=pltpu.VMEM)
    smem = pl.BlockSpec(memory_space=pltpu.SMEM)
    dma = pltpu.SemaphoreType.DMA
    gd, oh, sc, gg, loss = pl.pallas_call(
        gather_kernel,
        name="pool_gather",
        out_shape=(
            jax.ShapeDtypeStruct((2 * DOCS, D), BF16),
            jax.ShapeDtypeStruct((TOK, 128), BF16),
            jax.ShapeDtypeStruct((TOK, 128), F32),
            jax.ShapeDtypeStruct((1, D), F32),
            jax.ShapeDtypeStruct((1, 128), F32),
        ),
        in_specs=[pl.BlockSpec(memory_space=pl.ANY), vmem, smem, vmem, smem],
        out_specs=(vmem,) * 5,
        scratch_shapes=[
            pltpu.VMEM((TOK, D), BF16),
            pltpu.VMEM((DOCS, D), BF16),
            pltpu.VMEM((N_CTX, DOCS, FB), BF16),
            pltpu.VMEM((N_DP, DOCS, D), BF16),
            pltpu.VMEM((1, 128), F32),
            pltpu.VMEM((N_CTX, 1, 128), F32),
            pltpu.VMEM((N_DP, 1, 128), F32),
            pltpu.VMEM((ALL, ALL), F32),
            pltpu.VMEM((ALL, ALL), BF16),
            pltpu.VMEM((ALL, FB), F32),
            dma((4,)),
            dma, dma((N_CTX,)), dma, dma((NZ,)), dma, dma((NX,)), dma, dma((N_CTX,)),
            dma, dma((NZ,)), dma, dma((15,)), dma, dma((60,)), dma, dma,
        ],
        compiler_params=pltpu.CompilerParams(collective_id=0, has_side_effects=True),
    )(hidden[0], segments, positives, gain.reshape(1, D), inv_temp.reshape(1))

    rows = 64
    whole = lambda shape: pl.BlockSpec(shape, lambda i: (0, 0))
    grad_hidden, grad_gain, loss = pl.pallas_call(
        final_kernel,
        name="grad_hidden",
        grid=(TOK // rows,),
        out_shape=(
            jax.ShapeDtypeStruct((1, TOK, D), BF16),
            jax.ShapeDtypeStruct((1, D), F32),
            jax.ShapeDtypeStruct((1, 128), F32),
        ),
        in_specs=[
            pl.BlockSpec((1, rows, D), lambda i: (0, i, 0)),
            whole((2 * DOCS, D)),
            pl.BlockSpec((rows, 128), lambda i: (i, 0)),
            pl.BlockSpec((rows, 128), lambda i: (i, 0)),
            whole((1, D)),
            whole((1, 128)),
        ],
        out_specs=(pl.BlockSpec((1, rows, D), lambda i: (0, i, 0)), whole((1, D)), whole((1, 128))),
        scratch_shapes=[pltpu.VMEM((rows, D), F32)],
    )(hidden, gd, oh, sc, gg, loss)
    return grad_hidden, grad_gain.reshape(D), loss[0, 0]


def solution(mesh):
    return jax.shard_map(
        body,
        mesh=mesh,
        in_specs=(P("dp", "ctx", None), P("dp", "ctx"), P(), P(), P(("dp", "ctx"))),
        out_specs=(P("dp", "ctx", None), P(), P()),
        check_vma=False,
    )
```

```python
import functools

import jax
import jax.numpy as jnp
from jax import lax
from jax.experimental import pallas as pl
from jax.experimental.pallas import tpu as pltpu
from jax.sharding import PartitionSpec as P

MESH = pl.DeviceIdType.MESH
F32 = jnp.float32
BF16 = jnp.bfloat16

NX, NY, NZ = 4, 4, 8
N_DP, N_CTX = NX * NZ, NY * 2
DOCS = 16
ALL = N_DP * DOCS
TOK = 256
D = 4096
FB = D // N_CTX
HALF = ALL // 2
ROWS = 32
RB = 128


def mod(a, n):
    return lax.rem(a, n)


def dot(a, b, dims):
    return lax.dot_general(a, b, (dims, ((), ())), preferred_element_type=F32)


def gather_kernel(
    h_hbm, seg_hbm, pos_ref, gain_hbm, it_ref,
    gd_ref, oh_ref, sc_ref, gg_ref, loss_ref, h,
    seg_ref, gain_ref, part, recv, emb, meta_own, meta_ctx, meta, gram, nmat,
    in_sem, h_sem, m1_send, m1_recv, mz_send, mz_recv, mx_send, mx_recv, p1_send, p1_recv,
    z_send, z_recv, a_send, a_recv, b_send, b_recv, s_send, s_recv,
):
    dp, ctx = lax.axis_index("dp"), lax.axis_index("ctx")
    x, z = lax.div(dp, NZ), mod(dp, NZ)
    y, c = lax.div(ctx, 2), mod(ctx, 2)
    a = (1 - c) * x + c * y
    b = (1 - c) * y + c * x

    seg_copy = pltpu.make_async_copy(seg_hbm, seg_ref, in_sem.at[0])
    seg_copy.start()
    h_copies = []
    for i in range(4):
        rows = pl.ds(i * (TOK // 4), TOK // 4)
        h_copies.append(pltpu.make_async_copy(h_hbm.at[rows], h.at[rows], h_sem.at[i]))
        h_copies[-1].start()
    gain_copy = pltpu.make_async_copy(gain_hbm, gain_ref, in_sem.at[1])
    gain_copy.start()

    def at_a(aa):
        return ((1 - c) * (aa * NZ + z) + c * dp, (1 - c) * ctx + c * (aa * 2 + c))

    def at_b(bb):
        return ((1 - c) * dp + c * (bb * NZ + z), (1 - c) * (bb * 2 + c) + c * ctx)

    sibling = (dp, ctx + 1 - 2 * c)

    barrier = pltpu.get_barrier_semaphore()
    peers = [(x * NZ + mod(z + k, NZ), ctx) for k in (2, 6, 1, 7)]
    peers += [(dp, mod(ctx + k, N_CTX)) for k in range(1, N_CTX)]
    peers += [(mod(x + k, NX) * NZ + z, ctx) for k in range(1, NX)]
    for peer in peers:
        pl.semaphore_signal(barrier, inc=1, device_id=peer, device_id_type=MESH)

    seg_copy.wait()
    seg = seg_ref[...]
    doc_rows = lax.broadcasted_iota(jnp.int32, (DOCS, TOK), 0)
    onehot = (seg == doc_rows).astype(F32)
    lane = lax.broadcasted_iota(jnp.int32, (DOCS, 128), 1)
    counts = jnp.where(
        lane == DOCS + lax.broadcasted_iota(jnp.int32, (DOCS, 128), 0), jnp.sum(onehot, axis=1, keepdims=True), 0.0
    )
    lane1 = lax.broadcasted_iota(jnp.int32, (1, 128), 1)
    pos = jnp.where(lane1 == 2 * ctx, pos_ref[0], jnp.where(lane1 == 2 * ctx + 1, pos_ref[1], 0))
    meta_own[...] = pos.astype(F32) + jnp.sum(counts, axis=0, keepdims=True)

    squares = []
    for i in range(4):
        h_copies[i].wait()
        acc = jnp.zeros((TOK // 4, 128), F32)
        for j in range(D // 128):
            v = h[i * (TOK // 4):(i + 1) * (TOK // 4), j * 128:(j + 1) * 128].astype(F32)
            acc = acc + v * v
        squares.append(jnp.sum(acc, axis=1, keepdims=True))
    mean_sq = jnp.concatenate(squares, axis=0) * (1.0 / D)
    scale = jnp.broadcast_to(lax.rsqrt(mean_sq + 1e-06), (TOK, 128))
    sc_ref[...] = scale
    weight = onehot * jnp.transpose(scale)[0:DOCS, :]
    w_hi = weight.astype(BF16)
    w_lo = (weight - w_hi.astype(F32)).astype(BF16)
    w2 = jnp.concatenate([w_hi, w_lo], axis=0)
    gain_copy.wait()

    def p1(src, dst):
        return pltpu.make_async_remote_copy(
            src_ref=part.at[:, pl.ds(pl.multiple_of(dst * FB, FB), FB)], dst_ref=recv.at[src],
            send_sem=p1_send, recv_sem=p1_recv.at[src], device_id=(dp, dst), device_id_type=MESH,
        )

    def m1(src, dst):
        return pltpu.make_async_remote_copy(
            src_ref=meta_own, dst_ref=meta_ctx.at[src],
            send_sem=m1_send, recv_sem=m1_recv.at[src], device_id=(dp, dst), device_id_type=MESH,
        )

    for j in range(N_CTX):
        cols = slice(j * FB, (j + 1) * FB)
        both = dot(w2, h[:, cols], ((1,), (0,)))
        part[:, cols] = ((both[0:DOCS] + both[DOCS:]) * gain_ref[:, cols]).astype(BF16)

    pl.semaphore_wait(barrier, len(peers))
    others = [mod(ctx + k, N_CTX) for k in (4, 5, 3, 2, 6, 7, 1)]
    for other in others:
        p1(ctx, other).start()
    for other in others:
        m1(ctx, other).start()

    my_col = pl.ds(pl.multiple_of(ctx * FB, FB), FB)
    total = part[:, my_col].astype(F32)
    for other in reversed(others):
        p1(other, ctx).wait_recv()
        total = total + recv[other].astype(F32)
    emb[dp, :, my_col] = total.astype(BF16)

    def zcopy(zz, dst):
        ref = emb.at[x * NZ + zz, :, my_col]
        return pltpu.make_async_remote_copy(
            src_ref=ref, dst_ref=ref, send_sem=z_send, recv_sem=z_recv.at[zz],
            device_id=(x * NZ + dst, ctx), device_id_type=MESH,
        )

    def mz(zz, dst):
        ref = meta.at[x * NZ + zz]
        return pltpu.make_async_remote_copy(
            src_ref=ref, dst_ref=ref, send_sem=mz_send, recv_sem=mz_recv.at[zz],
            device_id=(x * NZ + dst, ctx), device_id_type=MESH,
        )

    def mx(xx, dst):
        ref = meta.at[pl.ds(xx * NZ, NZ)]
        return pltpu.make_async_remote_copy(
            src_ref=ref, dst_ref=ref, send_sem=mx_send, recv_sem=mx_recv.at[xx],
            device_id=(dst * NZ + z, ctx), device_id_type=MESH,
        )

    odd = mod(z, 2)
    z_off = lambda k: mod(z + k + NZ, NZ)
    pair_off = lambda k: 2 * mod(lax.div(z, 2) + k, NZ // 2)
    first = [z, z + 1 - 2 * odd, pair_off(3 - 2 * odd), pair_off(1 + 2 * odd), pair_off(2)]
    size = [1, 1, 2, 2, 2]

    def z_own(copy):
        for k in (1, -1, 2, -2):
            copy(z, z_off(k)).start()

    def z_near(copy):
        for k in (1, -1):
            copy(z_off(k), z).wait_recv()
            copy(z_off(k), z_off(-2 * k)).start()

    def z_next(copy):
        way = 2 - 4 * odd
        for k in (2, -2):
            copy(z_off(k), z).wait_recv()
        copy(z_off(way), z_off(-way)).start()

    def z_far(copy, ks):
        for k in ks:
            copy(z_off(k), z).wait_recv()

    a_off = lambda k: mod(a + k, NX)
    b_off = lambda k: mod(b + k, NX)

    def block(aa, bb, g):
        xx = (1 - c) * aa + c * bb
        yy = (1 - c) * bb + c * aa
        col = pl.multiple_of((yy * 2 + c) * FB, FB)
        return emb.at[pl.ds(xx * NZ + first[g], size[g]), :, pl.ds(col, FB)]

    def acopy(am, g, way, to):
        ref = block(a_off(am), b, g)
        return pltpu.make_async_remote_copy(
            src_ref=ref, dst_ref=ref, send_sem=a_send, recv_sem=a_recv.at[3 * g + way],
            device_id=at_a(to), device_id_type=MESH,
        )

    def bcopy(am, bm, g, way, to):
        ref = block(a_off(am), b_off(bm), g)
        return pltpu.make_async_remote_copy(
            src_ref=ref, dst_ref=ref, send_sem=b_send, recv_sem=b_recv.at[12 * g + 3 * am + way],
            device_id=at_b(to), device_id_type=MESH,
        )

    def sib(am, bm, g):
        ref = block(a_off(am), b_off(bm), g)
        pltpu.make_async_remote_copy(
            src_ref=ref, dst_ref=ref, send_sem=s_send, recv_sem=s_recv,
            device_id=sibling, device_id_type=MESH,
        ).start()

    def spread(am, g):
        bcopy(am, 0, g, 0, b_off(1)).start()
        bcopy(am, 0, g, 1, b_off(3)).start()
        sib(am, 0, g)

    def enter(g):
        for way, k in ((0, 1), (1, 3), (2, 2)):
            acopy(0, g, way, a_off(k)).start()
        spread(0, g)

    def along_a(g):
        for way, k in ((0, 3), (1, 1), (2, 2)):
            acopy(k, g, way, a).wait_recv()
            spread(k, g)

    def relay(am, g):
        bcopy(am, 3, g, 0, b).wait_recv()
        bcopy(am, 1, g, 1, b).wait_recv()
        if (g + (am >= 2)) % 2 == 0:
            bcopy(am, 3, g, 2, b_off(1)).start()
        else:
            bcopy(am, 1, g, 2, b_off(3)).start()
        sib(am, 3, g)
        sib(am, 1, g)

    def last(am, g):
        bcopy(am, 2, g, 2, b).wait_recv()
        sib(am, 2, g)

    z_own(zcopy)
    enter(0)
    meta_sum = meta_own[...]
    for other in others:
        m1(other, ctx).wait_recv()
        meta_sum = meta_sum + meta_ctx[other]
    meta[dp] = meta_sum
    z_own(mz)

    z_near(zcopy)
    enter(1)
    along_a(0)
    z_next(zcopy)
    enter(2)
    relay(0, 0)
    along_a(1)
    z_far(zcopy, (3, -3))
    enter(3)
    relay(0, 1)
    z_near(mz)
    along_a(2)
    z_far(zcopy, (4,))
    enter(4)
    z_next(mz)
    for am in (3, 1, 2):
        relay(am, 0)
    last(0, 0)
    along_a(3)
    for am in (3, 1, 2):
        relay(am, 1)
    relay(0, 2)
    z_far(mz, (3, -3, 4))
    for k in range(1, NX):
        mx(x, mod(x + k, NX)).start()
    along_a(4)
    for am in (3, 1, 2):
        last(am, 0)
    last(0, 1)
    relay(0, 3)
    for am in (3, 1, 2):
        relay(am, 2)
    relay(0, 4)
    for am in (3, 1, 2):
        last(am, 1)
    last(0, 2)
    for am in (3, 1, 2):
        relay(am, 3)
    last(0, 3)
    for am in (3, 1, 2):
        relay(am, 4)
    for am in (3, 1, 2):
        last(am, 2)
    for g in (3, 4):
        for am in (0, 3, 1, 2):
            if (am, g) != (0, 3):
                last(am, g)

    gram[...] = jnp.zeros_like(gram)

    def gram_of(core):
        @pl.loop(0, NY)
        def _(yy):
            col = pl.multiple_of((yy * 2 + core) * FB, FB)
            e = emb[:, :, pl.ds(col, FB)].reshape(ALL, FB)
            gram[...] += dot(e, e, ((1,), (1,)))

    gram_of(c)
    pltpu.make_async_remote_copy(
        src_ref=emb.at[pl.ds(0, N_DP // 2)], dst_ref=emb.at[pl.ds(0, N_DP // 2)],
        send_sem=s_send, recv_sem=s_recv, device_id=sibling, device_id_type=MESH,
    ).wait_recv()
    gram_of(1 - c)

    for k in range(1, NX):
        mx(mod(x + k, NX), x).wait_recv()

    inv_temp = it_ref[0]
    info = jnp.broadcast_to(meta[...], (N_DP, DOCS, 128)).reshape(ALL, 128)
    at = lax.broadcasted_iota(jnp.int32, (ALL, 128), 1) - mod(lax.broadcasted_iota(jnp.int32, (ALL, 128), 0), DOCS)
    pos_f = jnp.sum(jnp.where(at == 0, info, 0.0), axis=1, keepdims=True)
    pos_col = pos_f.astype(jnp.int32)
    count_col = jnp.sum(jnp.where(at == DOCS, info, 0.0), axis=1, keepdims=True)
    eye = lax.broadcasted_iota(jnp.int32, (RB, RB), 0) == lax.broadcasted_iota(jnp.int32, (RB, RB), 1)
    blocks = [slice(i * RB, (i + 1) * RB) for i in range(ALL // RB)]

    def as_row(cols):
        return jnp.concatenate(
            [jnp.sum(jnp.where(eye, jnp.broadcast_to(v, (RB, RB)), 0.0), axis=0, keepdims=True) for v in cols],
            axis=1,
        )

    q_cols = []
    for r in blocks:
        norm2 = jnp.sum(jnp.where(eye, gram[r, r], 0.0), axis=1, keepdims=True)
        inv_count = 1.0 / count_col[r]
        q_cols.append(inv_count * lax.rsqrt(norm2 * inv_count * inv_count + 1e-06))
    q_row = as_row(q_cols)
    pos_row = as_row([pos_f[r] for r in blocks]).astype(jnp.int32)

    lane_all = lax.broadcasted_iota(jnp.int32, (RB, ALL), 1)
    sub_all = lax.broadcasted_iota(jnp.int32, (RB, ALL), 0)
    lse_cols = []
    loss = jnp.zeros((1, 1), F32)
    for i, r in enumerate(blocks):
        cosine = gram[r, :] * q_cols[i] * q_row
        gram[r, :] = cosine
        logits = jnp.where(lane_all == sub_all + i * RB, -1e30, cosine * inv_temp)
        top = jnp.max(logits, axis=1, keepdims=True)
        sum_exp = jnp.sum(jnp.exp(logits - top), axis=1, keepdims=True)
        lse = top + jnp.log(sum_exp)
        at_pos = jnp.sum(jnp.where(lane_all == pos_col[r], logits, 0.0), axis=1, keepdims=True)
        loss = loss + jnp.sum(lse - at_pos, axis=0, keepdims=True)
        lse_cols.append(lse)
    loss_ref[...] = jnp.broadcast_to(loss * (1.0 / ALL), (1, 128))
    lse_row = as_row(lse_cols)

    for i, r in enumerate(blocks):
        cosine = gram[r, :]
        diagonal = lane_all == sub_all + i * RB
        logits = jnp.where(diagonal, -1e30, cosine * inv_temp)
        factor = inv_temp * (1.0 / ALL)
        own = (jnp.exp(logits - lse_cols[i]) - (lane_all == pos_col[r]).astype(F32)) * factor
        other = (jnp.exp(logits - lse_row) - (sub_all + i * RB == pos_row).astype(F32)) * factor
        both = own.astype(BF16).astype(F32) + other.astype(BF16).astype(F32)
        along = jnp.sum(both * cosine, axis=1, keepdims=True)
        grads = (both - jnp.where(diagonal, along, 0.0)) * q_cols[i] * q_row
        gram[r, :] = grads
        if i < 2:
            grads = jnp.where(lane_all < HALF, grads, 2.0 * grads)
        nmat[r, :] = grads.astype(BF16)

    n_own = gram[pl.ds(pl.multiple_of(dp * DOCS, DOCS), DOCS), :]
    n_hi = n_own.astype(BF16)
    n_own = jnp.concatenate([n_hi, (n_own - n_hi.astype(F32)).astype(BF16)], axis=0)
    n_top, n_low = nmat[0:HALF, :], nmat[HALF:, HALF:]
    for j in range(N_CTX):
        cols = slice(j * FB, (j + 1) * FB)
        e = emb[:, :, cols].reshape(ALL, FB)
        top = dot(n_top, e, ((1,), (0,))) * e[0:HALF].astype(F32)
        low = dot(n_low, e[HALF:], ((1,), (0,))) * e[HALF:].astype(F32)
        gain = gain_ref[:, cols]
        gg_ref[:, cols] = (jnp.sum(top, axis=0, keepdims=True) + jnp.sum(low, axis=0, keepdims=True)) / gain
        both = dot(n_own, e, ((1,), (0,)))
        g16 = (both[0:DOCS] + both[DOCS:]) * gain
        g_hi = g16.astype(BF16)
        gd_ref[0:DOCS, cols] = g_hi
        gd_ref[DOCS:, cols] = (g16 - g_hi.astype(F32)).astype(BF16)

    oh = jnp.concatenate([onehot, onehot, jnp.zeros((128 - 2 * DOCS, TOK), F32)], axis=0)
    oh_ref[...] = jnp.transpose(oh).astype(BF16)

    def sent(ref, sem):
        pltpu.make_async_remote_copy(
            src_ref=ref, dst_ref=ref, send_sem=sem, recv_sem=s_recv, device_id=sibling, device_id_type=MESH,
        ).wait_send()

    sent(recv.at[pl.ds(0, N_CTX - 1)], p1_send)
    sent(meta_ctx.at[pl.ds(0, N_CTX - 1)], m1_send)
    sent(emb.at[pl.ds(0, NZ - 1), :, pl.ds(0, FB)], z_send)
    sent(meta.at[pl.ds(0, NZ - 1)], mz_send)
    sent(meta.at[pl.ds(0, NZ * (NX - 1))], mx_send)
    sent(emb.at[pl.ds(0, 3)], a_send)
    sent(emb.at[pl.ds(0, 12)], b_send)
    sent(emb.at[pl.ds(0, 16)], s_send)


def final_kernel(h_ref, gd_ref, oh_ref, sc_ref, gg_ref, loss_ref, out_hbm, gg_out, loss_out, grad, out, sem):
    select = oh_ref[:, 0:2 * DOCS]
    for j in range(D // FB):
        cols = slice(j * FB, (j + 1) * FB)
        grad[:, cols] = dot(select, gd_ref[:, cols], ((1,), (0,)))
    copies = []
    for i in range(TOK // ROWS):
        r = slice(i * ROWS, (i + 1) * ROWS)
        acc = jnp.zeros((ROWS, 128), F32)
        for j in range(D // 128):
            cols = slice(j * 128, (j + 1) * 128)
            acc = acc + grad[r, cols] * h_ref[r, cols].astype(F32)
        inner = jnp.sum(acc, axis=1, keepdims=True) * (1.0 / D)
        scale = sc_ref[r, 0:1]
        coef = scale * scale * scale * inner
        for j in range(D // 512):
            cols = slice(j * 512, (j + 1) * 512)
            out[r, cols] = (scale * grad[r, cols] - h_ref[r, cols].astype(F32) * coef).astype(BF16)
        copies.append(pltpu.make_async_copy(out.at[pl.ds(i * ROWS, ROWS)], out_hbm.at[0, pl.ds(i * ROWS, ROWS)], sem.at[i]))
        copies[-1].start()
    gg_out[...] = gg_ref[...]
    loss_out[...] = loss_ref[...]
    for copy in copies:
        copy.wait()


def body(hidden, segments, gain, inv_temp, positives):
    hbm = lambda v: pltpu.with_memory_space_constraint(v, pltpu.HBM)
    vmem = pl.BlockSpec(memory_space=pltpu.VMEM)
    in_hbm = pl.BlockSpec(memory_space=pltpu.HBM)
    smem = pl.BlockSpec(memory_space=pltpu.SMEM)
    dma = pltpu.SemaphoreType.DMA
    gd, oh, sc, gg, loss, h = pl.pallas_call(
        gather_kernel,
        name="pool_gather",
        out_shape=(
            jax.ShapeDtypeStruct((2 * DOCS, D), BF16),
            jax.ShapeDtypeStruct((TOK, 128), BF16),
            jax.ShapeDtypeStruct((TOK, 128), F32),
            jax.ShapeDtypeStruct((1, D), F32),
            jax.ShapeDtypeStruct((1, 128), F32),
            jax.ShapeDtypeStruct((TOK, D), BF16),
        ),
        in_specs=[in_hbm, in_hbm, smem, in_hbm, smem],
        out_specs=(vmem,) * 6,
        scratch_shapes=[
            pltpu.VMEM((1, TOK), jnp.int32),
            pltpu.VMEM((1, D), F32),
            pltpu.VMEM((DOCS, D), BF16),
            pltpu.VMEM((N_CTX, DOCS, FB), BF16),
            pltpu.VMEM((N_DP, DOCS, D), BF16),
            pltpu.VMEM((1, 128), F32),
            pltpu.VMEM((N_CTX, 1, 128), F32),
            pltpu.VMEM((N_DP, 1, 128), F32),
            pltpu.VMEM((ALL, ALL), F32),
            pltpu.VMEM((ALL, ALL), BF16),
            dma((2,)),
            dma((4,)),
            dma, dma((N_CTX,)), dma, dma((NZ,)), dma, dma((NX,)), dma, dma((N_CTX,)),
            dma, dma((NZ,)), dma, dma((15,)), dma, dma((60,)), dma, dma,
        ],
        compiler_params=pltpu.CompilerParams(collective_id=0, has_side_effects=True, vmem_limit_bytes=20 << 20),
    )(hbm(hidden[0]), hbm(segments), hbm(positives), hbm(gain.reshape(1, D)), inv_temp.reshape(1))

    grad_hidden, grad_gain, loss = pl.pallas_call(
        final_kernel,
        name="grad_hidden",
        out_shape=(
            jax.ShapeDtypeStruct((1, TOK, D), BF16),
            jax.ShapeDtypeStruct((1, D), F32),
            jax.ShapeDtypeStruct((1, 128), F32),
        ),
        in_specs=[vmem] * 6,
        out_specs=(pl.BlockSpec(memory_space=pltpu.HBM), vmem, vmem),
        scratch_shapes=[pltpu.VMEM((TOK, D), F32), pltpu.VMEM((TOK, D), BF16), dma((TOK // ROWS,))],
        compiler_params=pltpu.CompilerParams(vmem_limit_bytes=20 << 20),
    )(h, gd, oh, sc, gg, loss)
    return grad_hidden, grad_gain.reshape(D), loss[0, 0]


def solution(mesh):
    return jax.shard_map(
        body,
        mesh=mesh,
        in_specs=(P("dp", "ctx", None), P("dp", "ctx"), P(), P(), P(("dp", "ctx"))),
        out_specs=(P("dp", "ctx", None), P(), P()),
        check_vma=False,
    )
```

```python
import functools

import jax
import jax.numpy as jnp
from jax import lax
from jax.experimental import pallas as pl
from jax.experimental.pallas import tpu as pltpu
from jax.sharding import PartitionSpec as P

MESH = pl.DeviceIdType.MESH
F32 = jnp.float32
BF16 = jnp.bfloat16

NX, NY, NZ = 4, 4, 8
N_DP, N_CTX = NX * NZ, NY * 2
DOCS = 16
ALL = N_DP * DOCS
TOK = 256
D = 4096
FB = D // N_CTX
HALF = ALL // 2
ROWS = 32
DIRECT = (3, 4)
RB = 128


def mod(a, n):
    return lax.rem(a, n)


def dot(a, b, dims):
    return lax.dot_general(a, b, (dims, ((), ())), preferred_element_type=F32)


def gather_kernel(
    h_hbm, seg_hbm, pos_ref, gain_hbm, it_ref,
    gd_ref, oh_ref, sc_ref, gg_ref, loss_ref, h,
    seg_ref, gain_ref, part, recv, emb, meta_own, meta_ctx, meta, gram, nmat,
    in_sem, h_sem, m1_send, m1_recv, mz_send, mz_recv, mx_send, mx_recv, p1_send, p1_recv,
    z_send, z_recv, a_send, a_recv, b_send, b_recv, s_send, s_recv,
):
    dp, ctx = lax.axis_index("dp"), lax.axis_index("ctx")
    x, z = lax.div(dp, NZ), mod(dp, NZ)
    y, c = lax.div(ctx, 2), mod(ctx, 2)
    a = (1 - c) * x + c * y
    b = (1 - c) * y + c * x

    seg_copy = pltpu.make_async_copy(seg_hbm, seg_ref, in_sem.at[0])
    seg_copy.start()
    h_copies = []
    for i in range(4):
        rows = pl.ds(i * (TOK // 4), TOK // 4)
        h_copies.append(pltpu.make_async_copy(h_hbm.at[rows], h.at[rows], h_sem.at[i]))
        h_copies[-1].start()
    gain_copy = pltpu.make_async_copy(gain_hbm, gain_ref, in_sem.at[1])
    gain_copy.start()

    def at_a(aa):
        return ((1 - c) * (aa * NZ + z) + c * dp, (1 - c) * ctx + c * (aa * 2 + c))

    def at_b(bb):
        return ((1 - c) * dp + c * (bb * NZ + z), (1 - c) * (bb * 2 + c) + c * ctx)

    sibling = (dp, ctx + 1 - 2 * c)

    barrier = pltpu.get_barrier_semaphore()
    peers = [(x * NZ + mod(z + k, NZ), ctx) for k in (2, 6, 1, 7)]
    peers += [(dp, mod(ctx + k, N_CTX)) for k in range(1, N_CTX)]
    peers += [(mod(x + k, NX) * NZ + z, ctx) for k in range(1, NX)]
    for peer in peers:
        pl.semaphore_signal(barrier, inc=1, device_id=peer, device_id_type=MESH)

    seg_copy.wait()
    seg = seg_ref[...]
    doc_rows = lax.broadcasted_iota(jnp.int32, (DOCS, TOK), 0)
    onehot = (seg == doc_rows).astype(F32)
    lane = lax.broadcasted_iota(jnp.int32, (DOCS, 128), 1)
    counts = jnp.where(
        lane == DOCS + lax.broadcasted_iota(jnp.int32, (DOCS, 128), 0), jnp.sum(onehot, axis=1, keepdims=True), 0.0
    )
    lane1 = lax.broadcasted_iota(jnp.int32, (1, 128), 1)
    pos = jnp.where(lane1 == 2 * ctx, pos_ref[0], jnp.where(lane1 == 2 * ctx + 1, pos_ref[1], 0))
    meta_own[...] = pos.astype(F32) + jnp.sum(counts, axis=0, keepdims=True)

    squares = []
    for i in range(4):
        h_copies[i].wait()
        acc = jnp.zeros((TOK // 4, 128), F32)
        for j in range(D // 128):
            v = h[i * (TOK // 4):(i + 1) * (TOK // 4), j * 128:(j + 1) * 128].astype(F32)
            acc = acc + v * v
        squares.append(jnp.sum(acc, axis=1, keepdims=True))
    mean_sq = jnp.concatenate(squares, axis=0) * (1.0 / D)
    scale = jnp.broadcast_to(lax.rsqrt(mean_sq + 1e-06), (TOK, 128))
    sc_ref[...] = scale
    weight = onehot * jnp.transpose(scale)[0:DOCS, :]
    w_hi = weight.astype(BF16)
    w_lo = (weight - w_hi.astype(F32)).astype(BF16)
    w2 = jnp.concatenate([w_hi, w_lo], axis=0)
    gain_copy.wait()

    def p1(src, dst):
        return pltpu.make_async_remote_copy(
            src_ref=part.at[:, pl.ds(pl.multiple_of(dst * FB, FB), FB)], dst_ref=recv.at[src],
            send_sem=p1_send, recv_sem=p1_recv.at[src], device_id=(dp, dst), device_id_type=MESH,
        )

    def m1(src, dst):
        return pltpu.make_async_remote_copy(
            src_ref=meta_own, dst_ref=meta_ctx.at[src],
            send_sem=m1_send, recv_sem=m1_recv.at[src], device_id=(dp, dst), device_id_type=MESH,
        )

    for j in range(N_CTX):
        cols = slice(j * FB, (j + 1) * FB)
        both = dot(w2, h[:, cols], ((1,), (0,)))
        part[:, cols] = ((both[0:DOCS] + both[DOCS:]) * gain_ref[:, cols]).astype(BF16)

    pl.semaphore_wait(barrier, len(peers))
    others = [mod(ctx + k, N_CTX) for k in (4, 5, 3, 2, 6, 7, 1)]
    for other in others:
        p1(ctx, other).start()
    for other in others:
        m1(ctx, other).start()

    my_col = pl.ds(pl.multiple_of(ctx * FB, FB), FB)
    total = part[:, my_col].astype(F32)
    for other in reversed(others):
        p1(other, ctx).wait_recv()
        total = total + recv[other].astype(F32)
    emb[dp, :, my_col] = total.astype(BF16)

    def zcopy(zz, dst):
        ref = emb.at[x * NZ + zz, :, my_col]
        return pltpu.make_async_remote_copy(
            src_ref=ref, dst_ref=ref, send_sem=z_send, recv_sem=z_recv.at[zz],
            device_id=(x * NZ + dst, ctx), device_id_type=MESH,
        )

    def mz(zz, dst):
        ref = meta.at[x * NZ + zz]
        return pltpu.make_async_remote_copy(
            src_ref=ref, dst_ref=ref, send_sem=mz_send, recv_sem=mz_recv.at[zz],
            device_id=(x * NZ + dst, ctx), device_id_type=MESH,
        )

    def mx(xx, dst):
        ref = meta.at[pl.ds(xx * NZ, NZ)]
        return pltpu.make_async_remote_copy(
            src_ref=ref, dst_ref=ref, send_sem=mx_send, recv_sem=mx_recv.at[xx],
            device_id=(dst * NZ + z, ctx), device_id_type=MESH,
        )

    odd = mod(z, 2)
    z_off = lambda k: mod(z + k + NZ, NZ)
    pair_off = lambda k: 2 * mod(lax.div(z, 2) + k, NZ // 2)
    first = [z, z + 1 - 2 * odd, pair_off(3 - 2 * odd), pair_off(1 + 2 * odd), pair_off(2)]
    size = [1, 1, 2, 2, 2]

    def z_own(copy):
        for k in (1, -1, 2, -2):
            copy(z, z_off(k)).start()

    def z_near(copy):
        for k in (1, -1):
            copy(z_off(k), z).wait_recv()
            copy(z_off(k), z_off(-2 * k)).start()

    def z_next(copy):
        way = 2 - 4 * odd
        for k in (2, -2):
            copy(z_off(k), z).wait_recv()
        copy(z_off(way), z_off(-way)).start()

    def z_far(copy, ks):
        for k in ks:
            copy(z_off(k), z).wait_recv()

    a_off = lambda k: mod(a + k, NX)
    b_off = lambda k: mod(b + k, NX)

    def block(aa, bb, g):
        xx = (1 - c) * aa + c * bb
        yy = (1 - c) * bb + c * aa
        col = pl.multiple_of((yy * 2 + c) * FB, FB)
        return emb.at[pl.ds(xx * NZ + first[g], size[g]), :, pl.ds(col, FB)]

    def acopy(am, g, way, to):
        ref = block(a_off(am), b, g)
        return pltpu.make_async_remote_copy(
            src_ref=ref, dst_ref=ref, send_sem=a_send, recv_sem=a_recv.at[3 * g + way],
            device_id=at_a(to), device_id_type=MESH,
        )

    def bcopy(am, bm, g, way, to):
        ref = block(a_off(am), b_off(bm), g)
        return pltpu.make_async_remote_copy(
            src_ref=ref, dst_ref=ref, send_sem=b_send, recv_sem=b_recv.at[12 * g + 3 * am + way],
            device_id=at_b(to), device_id_type=MESH,
        )

    def sib(am, bm, g):
        ref = block(a_off(am), b_off(bm), g)
        pltpu.make_async_remote_copy(
            src_ref=ref, dst_ref=ref, send_sem=s_send, recv_sem=s_recv,
            device_id=sibling, device_id_type=MESH,
        ).start()

    def spread(am, g):
        bcopy(am, 0, g, 0, b_off(1)).start()
        bcopy(am, 0, g, 1, b_off(3)).start()
        if g in DIRECT:
            bcopy(am, 0, g, 2, b_off(2)).start()
        sib(am, 0, g)

    def enter(g):
        for way, k in ((0, 1), (1, 3), (2, 2)):
            acopy(0, g, way, a_off(k)).start()
        spread(0, g)

    def along_a(g):
        for way, k in ((0, 3), (1, 1), (2, 2)):
            acopy(k, g, way, a).wait_recv()
            spread(k, g)

    def relay(am, g):
        bcopy(am, 3, g, 0, b).wait_recv()
        bcopy(am, 1, g, 1, b).wait_recv()
        if g in DIRECT:
            pass
        elif (g + (am >= 2)) % 2 == 0:
            bcopy(am, 3, g, 2, b_off(1)).start()
        else:
            bcopy(am, 1, g, 2, b_off(3)).start()
        sib(am, 3, g)
        sib(am, 1, g)

    def last(am, g):
        bcopy(am, 2, g, 2, b).wait_recv()
        sib(am, 2, g)

    z_own(zcopy)
    enter(0)
    meta_sum = meta_own[...]
    for other in others:
        m1(other, ctx).wait_recv()
        meta_sum = meta_sum + meta_ctx[other]
    meta[dp] = meta_sum
    z_own(mz)
    z_near(zcopy)
    enter(1)
    z_near(mz)
    along_a(0)
    relay(0, 0)
    z_next(zcopy)
    enter(2)
    z_next(mz)
    along_a(1)
    z_far(zcopy, (3, -3))
    enter(3)
    relay(0, 1)
    along_a(2)
    z_far(zcopy, (4,))
    enter(4)
    z_far(mz, (3, -3, 4))
    for k in range(1, NX):
        mx(x, mod(x + k, NX)).start()
    relay(3, 0)
    relay(1, 0)
    relay(2, 0)
    along_a(3)
    relay(0, 2)
    last(0, 0)
    along_a(4)
    relay(3, 1)
    relay(1, 1)
    relay(2, 1)
    last(3, 0)
    last(1, 0)
    last(2, 0)
    relay(0, 3)
    last(0, 1)
    relay(3, 2)
    relay(1, 2)
    relay(2, 2)
    relay(0, 4)
    last(3, 1)
    last(1, 1)
    last(2, 1)
    last(0, 2)
    relay(3, 3)
    relay(1, 3)
    relay(2, 3)
    relay(3, 4)
    relay(1, 4)
    relay(2, 4)
    last(3, 2)
    last(1, 2)
    last(2, 2)
    last(0, 3)
    last(3, 3)
    last(1, 3)
    last(2, 3)
    last(0, 4)
    last(3, 4)
    last(1, 4)
    last(2, 4)

    def gram_of(core, first_time):
        for yy in range(NY):
            col = pl.multiple_of((yy * 2 + core) * FB, FB)
            e = emb[:, :, pl.ds(col, FB)].reshape(ALL, FB)
            top = dot(e[0:HALF], e, ((1,), (1,)))
            low = dot(e[HALF:], e[HALF:], ((1,), (1,)))
            if first_time and yy == 0:
                gram[0:HALF, :] = top
                gram[HALF:, HALF:] = low
            else:
                gram[0:HALF, :] += top
                gram[HALF:, HALF:] += low

    gram_of(c, True)
    pltpu.make_async_remote_copy(
        src_ref=emb.at[pl.ds(0, N_DP // 2)], dst_ref=emb.at[pl.ds(0, N_DP // 2)],
        send_sem=s_send, recv_sem=s_recv, device_id=sibling, device_id_type=MESH,
    ).wait_recv()
    gram_of(1 - c, False)
    gram[HALF:, 0:HALF] = jnp.transpose(gram[0:HALF, HALF:])

    for k in range(1, NX):
        mx(mod(x + k, NX), x).wait_recv()

    inv_temp = it_ref[0]
    info = jnp.broadcast_to(meta[...], (N_DP, DOCS, 128)).reshape(ALL, 128)
    at = lax.broadcasted_iota(jnp.int32, (ALL, 128), 1) - mod(lax.broadcasted_iota(jnp.int32, (ALL, 128), 0), DOCS)
    pos_f = jnp.sum(jnp.where(at == 0, info, 0.0), axis=1, keepdims=True)
    pos_col = pos_f.astype(jnp.int32)
    count_col = jnp.sum(jnp.where(at == DOCS, info, 0.0), axis=1, keepdims=True)
    eye = lax.broadcasted_iota(jnp.int32, (RB, RB), 0) == lax.broadcasted_iota(jnp.int32, (RB, RB), 1)
    blocks = [slice(i * RB, (i + 1) * RB) for i in range(ALL // RB)]

    def as_row(cols):
        return jnp.concatenate(
            [jnp.sum(jnp.where(eye, jnp.broadcast_to(v, (RB, RB)), 0.0), axis=0, keepdims=True) for v in cols],
            axis=1,
        )

    q_cols = []
    for r in blocks:
        norm2 = jnp.sum(jnp.where(eye, gram[r, r], 0.0), axis=1, keepdims=True)
        inv_count = 1.0 / count_col[r]
        q_cols.append(inv_count * lax.rsqrt(norm2 * inv_count * inv_count + 1e-06))
    q_row = as_row(q_cols)
    pos_row = as_row([pos_f[r] for r in blocks]).astype(jnp.int32)

    lane_all = lax.broadcasted_iota(jnp.int32, (RB, ALL), 1)
    sub_all = lax.broadcasted_iota(jnp.int32, (RB, ALL), 0)
    lse_cols = []
    loss = jnp.zeros((1, 1), F32)
    for i, r in enumerate(blocks):
        logits = gram[r, :] * (q_cols[i] * inv_temp) * q_row
        parts = [logits[:, q] for q in blocks]
        parts[i] = jnp.where(eye, -1e30, parts[i])
        logits = jnp.concatenate(parts, axis=1)
        gram[r, :] = logits
        top = jnp.max(logits, axis=1, keepdims=True)
        sum_exp = jnp.sum(jnp.exp(logits - top), axis=1, keepdims=True)
        lse = top + jnp.log(sum_exp)
        at_pos = jnp.sum(jnp.where(lane_all == pos_col[r], logits, 0.0), axis=1, keepdims=True)
        loss = loss + jnp.sum(lse - at_pos, axis=0, keepdims=True)
        lse_cols.append(lse)
    loss_ref[...] = jnp.broadcast_to(loss * (1.0 / ALL), (1, 128))

    factor = inv_temp * (1.0 / ALL)
    shift_cols = [lse - jnp.log(jnp.broadcast_to(factor, (RB, 1))) for lse in lse_cols]
    shift_row = as_row(shift_cols)
    for i, r in enumerate(blocks):
        logits = gram[r, :]
        own = jnp.exp(logits - shift_cols[i])
        own = jnp.where(lane_all == pos_col[r], own - factor, own)
        other = jnp.exp(logits - shift_row)
        other = jnp.where(sub_all == pos_row - i * RB, other - factor, other)
        both = own.astype(BF16).astype(F32) + other.astype(BF16).astype(F32)
        along = jnp.sum(both * logits, axis=1, keepdims=True) * (1.0 / inv_temp)
        parts = [both[:, q] for q in blocks]
        parts[i] = jnp.where(eye, -along, parts[i])
        grads = jnp.concatenate(parts, axis=1) * q_cols[i] * q_row
        gram[r, :] = grads
        if i < 2:
            grads = jnp.concatenate([grads[:, 0:HALF], 2.0 * grads[:, HALF:]], axis=1)
        nmat[r, :] = grads.astype(BF16)

    n_own = gram[pl.ds(pl.multiple_of(dp * DOCS, DOCS), DOCS), :]
    n_hi = n_own.astype(BF16)
    n_own = jnp.concatenate([n_hi, (n_own - n_hi.astype(F32)).astype(BF16)], axis=0)
    n_top, n_low = nmat[0:HALF, :], nmat[HALF:, HALF:]
    for j in range(N_CTX):
        cols = slice(j * FB, (j + 1) * FB)
        e = emb[:, :, cols].reshape(ALL, FB)
        top = dot(n_top, e, ((1,), (0,))) * e[0:HALF].astype(F32)
        low = dot(n_low, e[HALF:], ((1,), (0,))) * e[HALF:].astype(F32)
        gain = gain_ref[:, cols]
        gg_ref[:, cols] = (jnp.sum(top, axis=0, keepdims=True) + jnp.sum(low, axis=0, keepdims=True)) / gain
        both = dot(n_own, e, ((1,), (0,)))
        g16 = (both[0:DOCS] + both[DOCS:]) * gain
        g_hi = g16.astype(BF16)
        gd_ref[0:DOCS, cols] = g_hi
        gd_ref[DOCS:, cols] = (g16 - g_hi.astype(F32)).astype(BF16)

    oh = jnp.concatenate([onehot, onehot, jnp.zeros((128 - 2 * DOCS, TOK), F32)], axis=0)
    oh_ref[...] = jnp.transpose(oh).astype(BF16)

    def sent(ref, sem):
        pltpu.make_async_remote_copy(
            src_ref=ref, dst_ref=ref, send_sem=sem, recv_sem=s_recv, device_id=sibling, device_id_type=MESH,
        ).wait_send()

    sent(recv.at[pl.ds(0, N_CTX - 1)], p1_send)
    sent(meta_ctx.at[pl.ds(0, N_CTX - 1)], m1_send)
    sent(emb.at[pl.ds(0, NZ - 1), :, pl.ds(0, FB)], z_send)
    sent(meta.at[pl.ds(0, NZ - 1)], mz_send)
    sent(meta.at[pl.ds(0, NZ * (NX - 1))], mx_send)
    sent(emb.at[pl.ds(0, 3)], a_send)
    sent(emb.at[pl.ds(0, 12)], b_send)
    sent(emb.at[pl.ds(0, 16)], s_send)


def final_kernel(h_ref, gd_ref, oh_ref, sc_ref, gg_ref, loss_ref, out_hbm, gg_out, loss_out, grad, out, sem):
    select = oh_ref[:, 0:2 * DOCS]
    acc = jnp.zeros((TOK, 128), F32)
    for j in range(D // FB):
        cols = slice(j * FB, (j + 1) * FB)
        rows = dot(select, gd_ref[:, cols], ((1,), (0,)))
        grad[:, cols] = rows
        rows = rows * h_ref[:, cols].astype(F32)
        for k in range(FB // 128):
            acc = acc + rows[:, k * 128:(k + 1) * 128]
    inner_all = jnp.sum(acc, axis=1, keepdims=True) * (1.0 / D)
    copies = []
    for i in range(TOK // ROWS):
        r = slice(i * ROWS, (i + 1) * ROWS)
        inner = inner_all[r]
        scale = sc_ref[r, 0:1]
        coef = scale * scale * scale * inner
        for j in range(D // 512):
            cols = slice(j * 512, (j + 1) * 512)
            out[r, cols] = (scale * grad[r, cols] - h_ref[r, cols].astype(F32) * coef).astype(BF16)
        copies.append(pltpu.make_async_copy(out.at[pl.ds(i * ROWS, ROWS)], out_hbm.at[0, pl.ds(i * ROWS, ROWS)], sem.at[i]))
        copies[-1].start()
    gg_out[...] = gg_ref[...]
    loss_out[...] = loss_ref[...]
    for copy in copies:
        copy.wait()


def body(hidden, segments, gain, inv_temp, positives):
    hbm = lambda v: pltpu.with_memory_space_constraint(v, pltpu.HBM)
    vmem = pl.BlockSpec(memory_space=pltpu.VMEM)
    in_hbm = pl.BlockSpec(memory_space=pltpu.HBM)
    smem = pl.BlockSpec(memory_space=pltpu.SMEM)
    dma = pltpu.SemaphoreType.DMA
    gd, oh, sc, gg, loss, h = pl.pallas_call(
        gather_kernel,
        name="pool_gather",
        out_shape=(
            jax.ShapeDtypeStruct((2 * DOCS, D), BF16),
            jax.ShapeDtypeStruct((TOK, 128), BF16),
            jax.ShapeDtypeStruct((TOK, 128), F32),
            jax.ShapeDtypeStruct((1, D), F32),
            jax.ShapeDtypeStruct((1, 128), F32),
            jax.ShapeDtypeStruct((TOK, D), BF16),
        ),
        in_specs=[in_hbm, in_hbm, smem, in_hbm, smem],
        out_specs=(vmem,) * 6,
        scratch_shapes=[
            pltpu.VMEM((1, TOK), jnp.int32),
            pltpu.VMEM((1, D), F32),
            pltpu.VMEM((DOCS, D), BF16),
            pltpu.VMEM((N_CTX, DOCS, FB), BF16),
            pltpu.VMEM((N_DP, DOCS, D), BF16),
            pltpu.VMEM((1, 128), F32),
            pltpu.VMEM((N_CTX, 1, 128), F32),
            pltpu.VMEM((N_DP, 1, 128), F32),
            pltpu.VMEM((ALL, ALL), F32),
            pltpu.VMEM((ALL, ALL), BF16),
            dma((2,)),
            dma((4,)),
            dma, dma((N_CTX,)), dma, dma((NZ,)), dma, dma((NX,)), dma, dma((N_CTX,)),
            dma, dma((NZ,)), dma, dma((15,)), dma, dma((60,)), dma, dma,
        ],
        compiler_params=pltpu.CompilerParams(collective_id=0, has_side_effects=True, vmem_limit_bytes=20 << 20),
    )(hbm(hidden[0]), hbm(segments), hbm(positives), hbm(gain.reshape(1, D)), inv_temp.reshape(1))

    grad_hidden, grad_gain, loss = pl.pallas_call(
        final_kernel,
        name="grad_hidden",
        out_shape=(
            jax.ShapeDtypeStruct((1, TOK, D), BF16),
            jax.ShapeDtypeStruct((1, D), F32),
            jax.ShapeDtypeStruct((1, 128), F32),
        ),
        in_specs=[vmem] * 6,
        out_specs=(pl.BlockSpec(memory_space=pltpu.HBM), vmem, vmem),
        scratch_shapes=[pltpu.VMEM((TOK, D), F32), pltpu.VMEM((TOK, D), BF16), dma((TOK // ROWS,))],
        compiler_params=pltpu.CompilerParams(vmem_limit_bytes=20 << 20),
    )(h, gd, oh, sc, gg, loss)
    return grad_hidden, grad_gain.reshape(D), loss[0, 0]


def solution(mesh):
    return jax.shard_map(
        body,
        mesh=mesh,
        in_specs=(P("dp", "ctx", None), P("dp", "ctx"), P(), P(), P(("dp", "ctx"))),
        out_specs=(P("dp", "ctx", None), P(), P()),
        check_vma=False,
    )
```

```python
import functools

import jax
import jax.numpy as jnp
from jax import lax
from jax.experimental import pallas as pl
from jax.experimental.pallas import tpu as pltpu
from jax.sharding import PartitionSpec as P

MESH = pl.DeviceIdType.MESH
F32 = jnp.float32
BF16 = jnp.bfloat16

NX, NY, NZ = 4, 4, 8
N_DP, N_CTX = NX * NZ, NY * 2
DOCS = 16
ALL = N_DP * DOCS
TOK = 256
D = 4096
FB = D // N_CTX
HALF = ALL // 2
ROWS = 32
DIRECT = (4,)
RB = 128


def mod(a, n):
    return lax.rem(a, n)


def dot(a, b, dims):
    return lax.dot_general(a, b, (dims, ((), ())), preferred_element_type=F32)


def gather_kernel(
    h_hbm, seg_hbm, pos_ref, gain_hbm, it_ref,
    gd_ref, oh_ref, sc_ref, gg_ref, loss_ref, h,
    seg_ref, gain_ref, part, recv, emb, meta_own, meta_ctx, meta, gram, nmat,
    in_sem, h_sem, m1_send, m1_recv, mz_send, mz_recv, mx_send, mx_recv, p1_send, p1_recv,
    z_send, z_recv, a_send, a_recv, b_send, b_recv, s_send, s_recv,
):
    dp, ctx = lax.axis_index("dp"), lax.axis_index("ctx")
    x, z = lax.div(dp, NZ), mod(dp, NZ)
    y, c = lax.div(ctx, 2), mod(ctx, 2)
    a = (1 - c) * x + c * y
    b = (1 - c) * y + c * x

    seg_copy = pltpu.make_async_copy(seg_hbm, seg_ref, in_sem.at[0])
    seg_copy.start()
    h_copies = []
    for i in range(4):
        rows = pl.ds(i * (TOK // 4), TOK // 4)
        h_copies.append(pltpu.make_async_copy(h_hbm.at[rows], h.at[rows], h_sem.at[i]))
        h_copies[-1].start()
    gain_copy = pltpu.make_async_copy(gain_hbm, gain_ref, in_sem.at[1])
    gain_copy.start()

    def at_a(aa):
        return ((1 - c) * (aa * NZ + z) + c * dp, (1 - c) * ctx + c * (aa * 2 + c))

    def at_b(bb):
        return ((1 - c) * dp + c * (bb * NZ + z), (1 - c) * (bb * 2 + c) + c * ctx)

    sibling = (dp, ctx + 1 - 2 * c)

    barrier = pltpu.get_barrier_semaphore()
    peers = [(x * NZ + mod(z + k, NZ), ctx) for k in (2, 6, 1, 7)]
    peers += [(dp, mod(ctx + k, N_CTX)) for k in range(1, N_CTX)]
    peers += [(mod(x + k, NX) * NZ + z, ctx) for k in range(1, NX)]
    for peer in peers:
        pl.semaphore_signal(barrier, inc=1, device_id=peer, device_id_type=MESH)

    seg_copy.wait()
    seg = seg_ref[...]
    doc_rows = lax.broadcasted_iota(jnp.int32, (DOCS, TOK), 0)
    onehot = (seg == doc_rows).astype(F32)
    lane = lax.broadcasted_iota(jnp.int32, (DOCS, 128), 1)
    counts = jnp.where(
        lane == DOCS + lax.broadcasted_iota(jnp.int32, (DOCS, 128), 0), jnp.sum(onehot, axis=1, keepdims=True), 0.0
    )
    lane1 = lax.broadcasted_iota(jnp.int32, (1, 128), 1)
    pos = jnp.where(lane1 == 2 * ctx, pos_ref[0], jnp.where(lane1 == 2 * ctx + 1, pos_ref[1], 0))
    meta_own[...] = pos.astype(F32) + jnp.sum(counts, axis=0, keepdims=True)

    squares = []
    for i in range(4):
        h_copies[i].wait()
        acc = jnp.zeros((TOK // 4, 128), F32)
        for j in range(D // 128):
            v = h[i * (TOK // 4):(i + 1) * (TOK // 4), j * 128:(j + 1) * 128].astype(F32)
            acc = acc + v * v
        squares.append(jnp.sum(acc, axis=1, keepdims=True))
    mean_sq = jnp.concatenate(squares, axis=0) * (1.0 / D)
    scale = jnp.broadcast_to(lax.rsqrt(mean_sq + 1e-06), (TOK, 128))
    sc_ref[...] = scale
    weight = onehot * jnp.transpose(scale)[0:DOCS, :]
    w_hi = weight.astype(BF16)
    w_lo = (weight - w_hi.astype(F32)).astype(BF16)
    w2 = jnp.concatenate([w_hi, w_lo], axis=0)
    gain_copy.wait()

    def p1(src, dst):
        return pltpu.make_async_remote_copy(
            src_ref=part.at[:, pl.ds(pl.multiple_of(dst * FB, FB), FB)], dst_ref=recv.at[src],
            send_sem=p1_send, recv_sem=p1_recv.at[src], device_id=(dp, dst), device_id_type=MESH,
        )

    def m1(src, dst):
        return pltpu.make_async_remote_copy(
            src_ref=meta_own, dst_ref=meta_ctx.at[src],
            send_sem=m1_send, recv_sem=m1_recv.at[src], device_id=(dp, dst), device_id_type=MESH,
        )

    for j in range(N_CTX):
        cols = slice(j * FB, (j + 1) * FB)
        both = dot(w2, h[:, cols], ((1,), (0,)))
        part[:, cols] = ((both[0:DOCS] + both[DOCS:]) * gain_ref[:, cols]).astype(BF16)

    pl.semaphore_wait(barrier, len(peers))
    others = [mod(ctx + k, N_CTX) for k in (4, 5, 3, 2, 6, 7, 1)]
    for other in others:
        m1(ctx, other).start()
    for other in others:
        p1(ctx, other).start()

    my_col = pl.ds(pl.multiple_of(ctx * FB, FB), FB)

    def zcopy(zz, dst):
        ref = emb.at[x * NZ + zz, :, my_col]
        return pltpu.make_async_remote_copy(
            src_ref=ref, dst_ref=ref, send_sem=z_send, recv_sem=z_recv.at[zz],
            device_id=(x * NZ + dst, ctx), device_id_type=MESH,
        )

    def mz(zz, dst):
        ref = meta.at[x * NZ + zz]
        return pltpu.make_async_remote_copy(
            src_ref=ref, dst_ref=ref, send_sem=mz_send, recv_sem=mz_recv.at[zz],
            device_id=(x * NZ + dst, ctx), device_id_type=MESH,
        )

    def mx(xx, dst):
        ref = meta.at[pl.ds(xx * NZ, NZ)]
        return pltpu.make_async_remote_copy(
            src_ref=ref, dst_ref=ref, send_sem=mx_send, recv_sem=mx_recv.at[xx],
            device_id=(dst * NZ + z, ctx), device_id_type=MESH,
        )

    odd = mod(z, 2)
    z_off = lambda k: mod(z + k + NZ, NZ)
    pair_off = lambda k: 2 * mod(lax.div(z, 2) + k, NZ // 2)
    first = [z, z + 1 - 2 * odd, pair_off(3 - 2 * odd), pair_off(1 + 2 * odd), pair_off(2)]
    size = [1, 1, 2, 2, 2]

    def z_own(copy):
        for k in (1, -1, 2, -2):
            copy(z, z_off(k)).start()

    def z_near(copy):
        for k in (1, -1):
            copy(z_off(k), z).wait_recv()
            copy(z_off(k), z_off(-2 * k)).start()

    def z_next(copy):
        way = 2 - 4 * odd
        for k in (2, -2):
            copy(z_off(k), z).wait_recv()
        copy(z_off(way), z_off(-way)).start()

    def z_far(copy, ks):
        for k in ks:
            copy(z_off(k), z).wait_recv()

    a_off = lambda k: mod(a + k, NX)
    b_off = lambda k: mod(b + k, NX)

    def block(aa, bb, g):
        xx = (1 - c) * aa + c * bb
        yy = (1 - c) * bb + c * aa
        col = pl.multiple_of((yy * 2 + c) * FB, FB)
        return emb.at[pl.ds(xx * NZ + first[g], size[g]), :, pl.ds(col, FB)]

    def acopy(am, g, way, to):
        ref = block(a_off(am), b, g)
        return pltpu.make_async_remote_copy(
            src_ref=ref, dst_ref=ref, send_sem=a_send, recv_sem=a_recv.at[3 * g + way],
            device_id=at_a(to), device_id_type=MESH,
        )

    def bcopy(am, bm, g, way, to):
        ref = block(a_off(am), b_off(bm), g)
        return pltpu.make_async_remote_copy(
            src_ref=ref, dst_ref=ref, send_sem=b_send, recv_sem=b_recv.at[12 * g + 3 * am + way],
            device_id=at_b(to), device_id_type=MESH,
        )

    def sib(am, bm, g):
        ref = block(a_off(am), b_off(bm), g)
        pltpu.make_async_remote_copy(
            src_ref=ref, dst_ref=ref, send_sem=s_send, recv_sem=s_recv,
            device_id=sibling, device_id_type=MESH,
        ).start()

    def spread(am, g):
        bcopy(am, 0, g, 0, b_off(1)).start()
        bcopy(am, 0, g, 1, b_off(3)).start()
        if g in DIRECT:
            bcopy(am, 0, g, 2, b_off(2)).start()
        sib(am, 0, g)

    def enter(g):
        for way, k in ((0, 1), (1, 3), (2, 2)):
            acopy(0, g, way, a_off(k)).start()
        spread(0, g)

    def from_a(am, g):
        acopy(am, g, {3: 0, 1: 1, 2: 2}[am], a).wait_recv()
        spread(am, g)

    def from_b(am, bm, g):
        bcopy(am, bm, g, 0 if bm == 3 else 1, b).wait_recv()
        if g not in DIRECT and bm == (3 if (g + (am >= 2)) % 2 == 0 else 1):
            bcopy(am, bm, g, 2, b_off(4 - bm)).start()
        sib(am, bm, g)

    def last(am, g):
        bcopy(am, 2, g, 2, b).wait_recv()
        sib(am, 2, g)

    meta_sum = meta_own[...]
    for other in reversed(others):
        m1(other, ctx).wait_recv()
        meta_sum = meta_sum + meta_ctx[other]
    meta[dp] = meta_sum
    z_own(mz)
    total = part[:, my_col].astype(F32)
    for other in reversed(others):
        p1(other, ctx).wait_recv()
        total = total + recv[other].astype(F32)
    emb[dp, :, my_col] = total.astype(BF16)
    z_own(zcopy)
    enter(0)
    from_a(3, 0)
    from_a(1, 0)
    z_near(zcopy)
    z_near(mz)
    enter(1)
    from_b(0, 3, 0)
    from_b(0, 1, 0)
    from_a(2, 0)
    z_next(zcopy)
    z_next(mz)
    enter(2)
    from_b(3, 3, 0)
    from_b(3, 1, 0)
    from_b(1, 3, 0)
    from_b(1, 1, 0)
    from_a(3, 1)
    from_a(1, 1)
    from_b(0, 1, 1)
    z_far(zcopy, (3, -3))
    enter(3)
    from_b(0, 3, 1)
    from_b(2, 1, 0)
    last(0, 0)
    from_b(2, 3, 0)
    from_a(2, 1)
    from_a(1, 2)
    from_a(3, 2)
    from_b(0, 3, 2)
    last(1, 0)
    from_b(3, 3, 1)
    z_far(zcopy, (4,))
    enter(4)
    z_far(mz, (3, -3, 4))
    for k in range(1, NX):
        mx(x, mod(x + k, NX)).start()
    from_b(0, 1, 2)
    from_b(1, 3, 1)
    last(3, 0)
    from_a(2, 2)
    from_b(3, 1, 1)
    from_a(3, 3)
    from_b(1, 1, 1)
    last(0, 1)
    from_a(1, 3)
    from_b(0, 1, 3)
    from_b(0, 3, 3)
    last(2, 0)
    from_b(2, 3, 1)
    from_a(2, 3)
    from_b(2, 1, 1)
    from_b(1, 3, 2)
    from_b(1, 1, 2)
    from_b(3, 3, 2)
    from_b(3, 1, 2)
    last(0, 2)
    from_a(1, 4)
    last(3, 1)
    from_a(3, 4)
    from_b(0, 3, 4)
    from_b(0, 1, 4)
    from_b(2, 3, 2)
    from_a(2, 4)
    from_b(3, 3, 3)
    from_b(1, 3, 3)
    last(2, 1)
    from_b(2, 1, 2)
    last(0, 4)
    from_b(2, 3, 3)
    from_b(3, 1, 3)
    last(1, 1)
    last(1, 2)
    from_b(1, 1, 3)
    from_b(1, 3, 4)
    last(0, 3)
    from_b(2, 1, 3)
    last(3, 2)
    from_b(3, 3, 4)
    from_b(1, 1, 4)
    last(1, 4)
    from_b(3, 1, 4)
    from_b(2, 1, 4)
    from_b(2, 3, 4)
    last(3, 4)
    last(3, 3)
    last(2, 3)
    last(2, 2)
    last(2, 4)
    last(1, 3)

    def gram_of(core, first_time):
        for yy in range(NY):
            col = pl.multiple_of((yy * 2 + core) * FB, FB)
            e = emb[:, :, pl.ds(col, FB)].reshape(ALL, FB)
            top = dot(e[0:HALF], e, ((1,), (1,)))
            low = dot(e[HALF:], e[HALF:], ((1,), (1,)))
            if first_time and yy == 0:
                gram[0:HALF, :] = top
                gram[HALF:, HALF:] = low
            else:
                gram[0:HALF, :] += top
                gram[HALF:, HALF:] += low

    gram_of(c, True)
    pltpu.make_async_remote_copy(
        src_ref=emb.at[pl.ds(0, N_DP // 2)], dst_ref=emb.at[pl.ds(0, N_DP // 2)],
        send_sem=s_send, recv_sem=s_recv, device_id=sibling, device_id_type=MESH,
    ).wait_recv()
    gram_of(1 - c, False)
    gram[HALF:, 0:HALF] = jnp.transpose(gram[0:HALF, HALF:])

    for k in range(1, NX):
        mx(mod(x + k, NX), x).wait_recv()

    inv_temp = it_ref[0]
    info = jnp.broadcast_to(meta[...], (N_DP, DOCS, 128)).reshape(ALL, 128)
    at = lax.broadcasted_iota(jnp.int32, (ALL, 128), 1) - mod(lax.broadcasted_iota(jnp.int32, (ALL, 128), 0), DOCS)
    pos_f = jnp.sum(jnp.where(at == 0, info, 0.0), axis=1, keepdims=True)
    pos_col = pos_f.astype(jnp.int32)
    count_col = jnp.sum(jnp.where(at == DOCS, info, 0.0), axis=1, keepdims=True)
    eye = lax.broadcasted_iota(jnp.int32, (RB, RB), 0) == lax.broadcasted_iota(jnp.int32, (RB, RB), 1)
    blocks = [slice(i * RB, (i + 1) * RB) for i in range(ALL // RB)]

    def as_row(cols):
        return jnp.concatenate(
            [jnp.sum(jnp.where(eye, jnp.broadcast_to(v, (RB, RB)), 0.0), axis=0, keepdims=True) for v in cols],
            axis=1,
        )

    q_cols = []
    for r in blocks:
        norm2 = jnp.sum(jnp.where(eye, gram[r, r], 0.0), axis=1, keepdims=True)
        inv_count = 1.0 / count_col[r]
        q_cols.append(inv_count * lax.rsqrt(norm2 * inv_count * inv_count + 1e-06))
    q_row = as_row(q_cols)
    pos_row = as_row([pos_f[r] for r in blocks]).astype(jnp.int32)

    lane_all = lax.broadcasted_iota(jnp.int32, (RB, ALL), 1)
    sub_all = lax.broadcasted_iota(jnp.int32, (RB, ALL), 0)
    lse_cols = []
    loss = jnp.zeros((1, 1), F32)
    for i, r in enumerate(blocks):
        logits = gram[r, :] * (q_cols[i] * inv_temp) * q_row
        parts = [logits[:, q] for q in blocks]
        parts[i] = jnp.where(eye, -1e30, parts[i])
        logits = jnp.concatenate(parts, axis=1)
        gram[r, :] = logits
        top = jnp.max(logits, axis=1, keepdims=True)
        sum_exp = jnp.sum(jnp.exp(logits - top), axis=1, keepdims=True)
        lse = top + jnp.log(sum_exp)
        at_pos = jnp.sum(jnp.where(lane_all == pos_col[r], logits, 0.0), axis=1, keepdims=True)
        loss = loss + jnp.sum(lse - at_pos, axis=0, keepdims=True)
        lse_cols.append(lse)
    loss_ref[...] = jnp.broadcast_to(loss * (1.0 / ALL), (1, 128))

    factor = inv_temp * (1.0 / ALL)
    shift_cols = [lse - jnp.log(jnp.broadcast_to(factor, (RB, 1))) for lse in lse_cols]
    shift_row = as_row(shift_cols)
    for i, r in enumerate(blocks):
        logits = gram[r, :]
        own = jnp.exp(logits - shift_cols[i])
        own = jnp.where(lane_all == pos_col[r], own - factor, own)
        other = jnp.exp(logits - shift_row)
        other = jnp.where(sub_all == pos_row - i * RB, other - factor, other)
        both = own.astype(BF16).astype(F32) + other.astype(BF16).astype(F32)
        along = jnp.sum(both * logits, axis=1, keepdims=True) * (1.0 / inv_temp)
        parts = [both[:, q] for q in blocks]
        parts[i] = jnp.where(eye, -along, parts[i])
        grads = jnp.concatenate(parts, axis=1) * q_cols[i] * q_row
        gram[r, :] = grads
        if i < 2:
            grads = jnp.concatenate([grads[:, 0:HALF], 2.0 * grads[:, HALF:]], axis=1)
        nmat[r, :] = grads.astype(BF16)

    n_own = gram[pl.ds(pl.multiple_of(dp * DOCS, DOCS), DOCS), :]
    n_hi = n_own.astype(BF16)
    n_own = jnp.concatenate([n_hi, (n_own - n_hi.astype(F32)).astype(BF16)], axis=0)
    n_top, n_low = nmat[0:HALF, :], nmat[HALF:, HALF:]
    for j in range(N_CTX):
        cols = slice(j * FB, (j + 1) * FB)
        e = emb[:, :, cols].reshape(ALL, FB)
        top = dot(n_top, e, ((1,), (0,))) * e[0:HALF].astype(F32)
        low = dot(n_low, e[HALF:], ((1,), (0,))) * e[HALF:].astype(F32)
        gain = gain_ref[:, cols]
        gg_ref[:, cols] = (jnp.sum(top, axis=0, keepdims=True) + jnp.sum(low, axis=0, keepdims=True)) / gain
        both = dot(n_own, e, ((1,), (0,)))
        g16 = (both[0:DOCS] + both[DOCS:]) * gain
        g_hi = g16.astype(BF16)
        gd_ref[0:DOCS, cols] = g_hi
        gd_ref[DOCS:, cols] = (g16 - g_hi.astype(F32)).astype(BF16)

    oh = jnp.concatenate([onehot, onehot, jnp.zeros((128 - 2 * DOCS, TOK), F32)], axis=0)
    oh_ref[...] = jnp.transpose(oh).astype(BF16)

    def sent(ref, sem):
        pltpu.make_async_remote_copy(
            src_ref=ref, dst_ref=ref, send_sem=sem, recv_sem=s_recv, device_id=sibling, device_id_type=MESH,
        ).wait_send()

    sent(recv.at[pl.ds(0, N_CTX - 1)], p1_send)
    sent(meta_ctx.at[pl.ds(0, N_CTX - 1)], m1_send)
    sent(emb.at[pl.ds(0, NZ - 1), :, pl.ds(0, FB)], z_send)
    sent(meta.at[pl.ds(0, NZ - 1)], mz_send)
    sent(meta.at[pl.ds(0, NZ * (NX - 1))], mx_send)
    sent(emb.at[pl.ds(0, 3)], a_send)
    sent(emb.at[pl.ds(0, 12)], b_send)
    sent(emb.at[pl.ds(0, 16)], s_send)


def final_kernel(h_ref, gd_ref, oh_ref, sc_ref, gg_ref, loss_ref, out_hbm, gg_out, loss_out, grad, out, sem):
    select = oh_ref[:, 0:2 * DOCS]
    acc = jnp.zeros((TOK, 128), F32)
    for j in range(D // FB):
        cols = slice(j * FB, (j + 1) * FB)
        rows = dot(select, gd_ref[:, cols], ((1,), (0,)))
        grad[:, cols] = rows
        rows = rows * h_ref[:, cols].astype(F32)
        for k in range(FB // 128):
            acc = acc + rows[:, k * 128:(k + 1) * 128]
    inner_all = jnp.sum(acc, axis=1, keepdims=True) * (1.0 / D)
    copies = []
    for i in range(TOK // ROWS):
        r = slice(i * ROWS, (i + 1) * ROWS)
        inner = inner_all[r]
        scale = sc_ref[r, 0:1]
        coef = scale * scale * scale * inner
        for j in range(D // 512):
            cols = slice(j * 512, (j + 1) * 512)
            out[r, cols] = (scale * grad[r, cols] - h_ref[r, cols].astype(F32) * coef).astype(BF16)
        copies.append(pltpu.make_async_copy(out.at[pl.ds(i * ROWS, ROWS)], out_hbm.at[0, pl.ds(i * ROWS, ROWS)], sem.at[i]))
        copies[-1].start()
    gg_out[...] = gg_ref[...]
    loss_out[...] = loss_ref[...]
    for copy in copies:
        copy.wait()


def body(hidden, segments, gain, inv_temp, positives):
    hbm = lambda v: pltpu.with_memory_space_constraint(v, pltpu.HBM)
    vmem = pl.BlockSpec(memory_space=pltpu.VMEM)
    in_hbm = pl.BlockSpec(memory_space=pltpu.HBM)
    smem = pl.BlockSpec(memory_space=pltpu.SMEM)
    dma = pltpu.SemaphoreType.DMA
    gd, oh, sc, gg, loss, h = pl.pallas_call(
        gather_kernel,
        name="pool_gather",
        out_shape=(
            jax.ShapeDtypeStruct((2 * DOCS, D), BF16),
            jax.ShapeDtypeStruct((TOK, 128), BF16),
            jax.ShapeDtypeStruct((TOK, 128), F32),
            jax.ShapeDtypeStruct((1, D), F32),
            jax.ShapeDtypeStruct((1, 128), F32),
            jax.ShapeDtypeStruct((TOK, D), BF16),
        ),
        in_specs=[in_hbm, in_hbm, smem, in_hbm, smem],
        out_specs=(vmem,) * 6,
        scratch_shapes=[
            pltpu.VMEM((1, TOK), jnp.int32),
            pltpu.VMEM((1, D), F32),
            pltpu.VMEM((DOCS, D), BF16),
            pltpu.VMEM((N_CTX, DOCS, FB), BF16),
            pltpu.VMEM((N_DP, DOCS, D), BF16),
            pltpu.VMEM((1, 128), F32),
            pltpu.VMEM((N_CTX, 1, 128), F32),
            pltpu.VMEM((N_DP, 1, 128), F32),
            pltpu.VMEM((ALL, ALL), F32),
            pltpu.VMEM((ALL, ALL), BF16),
            dma((2,)),
            dma((4,)),
            dma, dma((N_CTX,)), dma, dma((NZ,)), dma, dma((NX,)), dma, dma((N_CTX,)),
            dma, dma((NZ,)), dma, dma((15,)), dma, dma((60,)), dma, dma,
        ],
        compiler_params=pltpu.CompilerParams(collective_id=0, has_side_effects=True, vmem_limit_bytes=20 << 20),
    )(hbm(hidden[0]), hbm(segments), hbm(positives), hbm(gain.reshape(1, D)), inv_temp.reshape(1))

    grad_hidden, grad_gain, loss = pl.pallas_call(
        final_kernel,
        name="grad_hidden",
        out_shape=(
            jax.ShapeDtypeStruct((1, TOK, D), BF16),
            jax.ShapeDtypeStruct((1, D), F32),
            jax.ShapeDtypeStruct((1, 128), F32),
        ),
        in_specs=[vmem] * 6,
        out_specs=(pl.BlockSpec(memory_space=pltpu.HBM), vmem, vmem),
        scratch_shapes=[pltpu.VMEM((TOK, D), F32), pltpu.VMEM((TOK, D), BF16), dma((TOK // ROWS,))],
        compiler_params=pltpu.CompilerParams(vmem_limit_bytes=20 << 20),
    )(h, gd, oh, sc, gg, loss)
    return grad_hidden, grad_gain.reshape(D), loss[0, 0]


def solution(mesh):
    return jax.shard_map(
        body,
        mesh=mesh,
        in_specs=(P("dp", "ctx", None), P("dp", "ctx"), P(), P(), P(("dp", "ctx"))),
        out_specs=(P("dp", "ctx", None), P(), P()),
        check_vma=False,
    )
```

```python
import functools

import jax
import jax.numpy as jnp
from jax import lax
from jax.experimental import pallas as pl
from jax.experimental.pallas import tpu as pltpu
from jax.sharding import PartitionSpec as P

MESH = pl.DeviceIdType.MESH
F32 = jnp.float32
BF16 = jnp.bfloat16

NX, NY, NZ = 4, 4, 8
N_DP, N_CTX = NX * NZ, NY * 2
DOCS = 16
ALL = N_DP * DOCS
TOK = 256
D = 4096
FB = D // N_CTX
HALF = ALL // 2
ROWS = 32
DIRECT = (5, 6, 7)
RB = 128


def mod(a, n):
    return lax.rem(a, n)


def dot(a, b, dims):
    return lax.dot_general(a, b, (dims, ((), ())), preferred_element_type=F32)


def gather_kernel(
    h_hbm, seg_hbm, pos_ref, gain_hbm, it_ref,
    gd_ref, oh_ref, sc_ref, gg_ref, loss_ref, h,
    seg_ref, gain_ref, part, recv, emb, meta_own, meta_ctx, meta, gram, nmat,
    in_sem, h_sem, m1_send, m1_recv, mz_send, mz_recv, mx_send, mx_recv, p1_send, p1_recv,
    z_send, z_recv, a_send, a_recv, b_send, b_recv, s_send, s_recv,
):
    dp, ctx = lax.axis_index("dp"), lax.axis_index("ctx")
    x, z = lax.div(dp, NZ), mod(dp, NZ)
    y, c = lax.div(ctx, 2), mod(ctx, 2)
    a = (1 - c) * x + c * y
    b = (1 - c) * y + c * x

    seg_copy = pltpu.make_async_copy(seg_hbm, seg_ref, in_sem.at[0])
    seg_copy.start()
    h_copies = []
    for i in range(4):
        rows = pl.ds(i * (TOK // 4), TOK // 4)
        h_copies.append(pltpu.make_async_copy(h_hbm.at[rows], h.at[rows], h_sem.at[i]))
        h_copies[-1].start()
    gain_copy = pltpu.make_async_copy(gain_hbm, gain_ref, in_sem.at[1])
    gain_copy.start()

    def at_a(aa):
        return ((1 - c) * (aa * NZ + z) + c * dp, (1 - c) * ctx + c * (aa * 2 + c))

    def at_b(bb):
        return ((1 - c) * dp + c * (bb * NZ + z), (1 - c) * (bb * 2 + c) + c * ctx)

    sibling = (dp, ctx + 1 - 2 * c)

    barrier = pltpu.get_barrier_semaphore()
    peers = [(x * NZ + mod(z + k, NZ), ctx) for k in (2, 6, 1, 7)]
    peers += [(dp, mod(ctx + k, N_CTX)) for k in range(1, N_CTX)]
    peers += [(mod(x + k, NX) * NZ + z, ctx) for k in range(1, NX)]
    for peer in peers:
        pl.semaphore_signal(barrier, inc=1, device_id=peer, device_id_type=MESH)

    seg_copy.wait()
    seg = seg_ref[...]
    doc_rows = lax.broadcasted_iota(jnp.int32, (DOCS, TOK), 0)
    onehot = (seg == doc_rows).astype(F32)
    lane = lax.broadcasted_iota(jnp.int32, (DOCS, 128), 1)
    counts = jnp.where(
        lane == DOCS + lax.broadcasted_iota(jnp.int32, (DOCS, 128), 0), jnp.sum(onehot, axis=1, keepdims=True), 0.0
    )
    lane1 = lax.broadcasted_iota(jnp.int32, (1, 128), 1)
    pos = jnp.where(lane1 == 2 * ctx, pos_ref[0], jnp.where(lane1 == 2 * ctx + 1, pos_ref[1], 0))
    meta_own[...] = pos.astype(F32) + jnp.sum(counts, axis=0, keepdims=True)

    squares = []
    for i in range(4):
        h_copies[i].wait()
        acc = jnp.zeros((TOK // 4, 128), F32)
        for j in range(D // 128):
            v = h[i * (TOK // 4):(i + 1) * (TOK // 4), j * 128:(j + 1) * 128].astype(F32)
            acc = acc + v * v
        squares.append(jnp.sum(acc, axis=1, keepdims=True))
    mean_sq = jnp.concatenate(squares, axis=0) * (1.0 / D)
    scale = jnp.broadcast_to(lax.rsqrt(mean_sq + 1e-06), (TOK, 128))
    sc_ref[...] = scale
    weight = onehot * jnp.transpose(scale)[0:DOCS, :]
    w_hi = weight.astype(BF16)
    w_lo = (weight - w_hi.astype(F32)).astype(BF16)
    w2 = jnp.concatenate([w_hi, w_lo], axis=0)
    gain_copy.wait()

    def p1(src, dst):
        return pltpu.make_async_remote_copy(
            src_ref=part.at[:, pl.ds(pl.multiple_of(dst * FB, FB), FB)], dst_ref=recv.at[src],
            send_sem=p1_send, recv_sem=p1_recv.at[src], device_id=(dp, dst), device_id_type=MESH,
        )

    def m1(src, dst):
        return pltpu.make_async_remote_copy(
            src_ref=meta_own, dst_ref=meta_ctx.at[src],
            send_sem=m1_send, recv_sem=m1_recv.at[src], device_id=(dp, dst), device_id_type=MESH,
        )

    for j in range(N_CTX):
        cols = slice(j * FB, (j + 1) * FB)
        both = dot(w2, h[:, cols], ((1,), (0,)))
        part[:, cols] = ((both[0:DOCS] + both[DOCS:]) * gain_ref[:, cols]).astype(BF16)

    pl.semaphore_wait(barrier, len(peers))
    others = [mod(ctx + k, N_CTX) for k in (4, 5, 3, 2, 6, 7, 1)]
    for other in others:
        m1(ctx, other).start()
    for other in others:
        p1(ctx, other).start()

    my_col = pl.ds(pl.multiple_of(ctx * FB, FB), FB)

    def zcopy(zz, dst):
        ref = emb.at[x * NZ + zz, :, my_col]
        return pltpu.make_async_remote_copy(
            src_ref=ref, dst_ref=ref, send_sem=z_send, recv_sem=z_recv.at[zz],
            device_id=(x * NZ + dst, ctx), device_id_type=MESH,
        )

    def mz(zz, dst):
        ref = meta.at[x * NZ + zz]
        return pltpu.make_async_remote_copy(
            src_ref=ref, dst_ref=ref, send_sem=mz_send, recv_sem=mz_recv.at[zz],
            device_id=(x * NZ + dst, ctx), device_id_type=MESH,
        )

    def mx(xx, dst):
        ref = meta.at[pl.ds(xx * NZ, NZ)]
        return pltpu.make_async_remote_copy(
            src_ref=ref, dst_ref=ref, send_sem=mx_send, recv_sem=mx_recv.at[xx],
            device_id=(dst * NZ + z, ctx), device_id_type=MESH,
        )

    odd = mod(z, 2)
    z_off = lambda k: mod(z + k + NZ, NZ)
    first = [z, z_off(1), z_off(-1), z_off(2), z_off(-2), z_off(3), z_off(-3), z_off(4)]
    size = [1] * NZ

    def z_own(copy):
        for k in (1, -1, 2, -2):
            copy(z, z_off(k)).start()

    def z_near(copy):
        for k in (1, -1):
            copy(z_off(k), z).wait_recv()
            copy(z_off(k), z_off(-2 * k)).start()

    def z_next(copy):
        way = 2 - 4 * odd
        for k in (2, -2):
            copy(z_off(k), z).wait_recv()
        copy(z_off(way), z_off(-way)).start()

    def z_far(copy, ks):
        for k in ks:
            copy(z_off(k), z).wait_recv()

    a_off = lambda k: mod(a + k, NX)
    b_off = lambda k: mod(b + k, NX)

    def block(aa, bb, g):
        xx = (1 - c) * aa + c * bb
        yy = (1 - c) * bb + c * aa
        col = pl.multiple_of((yy * 2 + c) * FB, FB)
        return emb.at[pl.ds(xx * NZ + first[g], size[g]), :, pl.ds(col, FB)]

    def acopy(am, g, way, to):
        ref = block(a_off(am), b, g)
        return pltpu.make_async_remote_copy(
            src_ref=ref, dst_ref=ref, send_sem=a_send, recv_sem=a_recv.at[3 * g + way],
            device_id=at_a(to), device_id_type=MESH,
        )

    def bcopy(am, bm, g, way, to):
        ref = block(a_off(am), b_off(bm), g)
        return pltpu.make_async_remote_copy(
            src_ref=ref, dst_ref=ref, send_sem=b_send, recv_sem=b_recv.at[12 * g + 3 * am + way],
            device_id=at_b(to), device_id_type=MESH,
        )

    def sib(am, bm, g):
        ref = block(a_off(am), b_off(bm), g)
        pltpu.make_async_remote_copy(
            src_ref=ref, dst_ref=ref, send_sem=s_send, recv_sem=s_recv,
            device_id=sibling, device_id_type=MESH,
        ).start()

    def spread(am, g):
        bcopy(am, 0, g, 0, b_off(1)).start()
        bcopy(am, 0, g, 1, b_off(3)).start()
        if g in DIRECT:
            bcopy(am, 0, g, 2, b_off(2)).start()
        sib(am, 0, g)

    def enter(g):
        for way, k in ((0, 1), (1, 3), (2, 2)):
            acopy(0, g, way, a_off(k)).start()
        spread(0, g)

    def from_a(am, g):
        acopy(am, g, {3: 0, 1: 1, 2: 2}[am], a).wait_recv()
        spread(am, g)

    def from_b(am, bm, g):
        bcopy(am, bm, g, 0 if bm == 3 else 1, b).wait_recv()
        if g not in DIRECT and bm == (3 if (g + (am >= 2)) % 2 == 0 else 1):
            bcopy(am, bm, g, 2, b_off(4 - bm)).start()
        sib(am, bm, g)

    def last(am, g):
        bcopy(am, 2, g, 2, b).wait_recv()
        sib(am, 2, g)

    meta_sum = meta_own[...]
    for other in reversed(others):
        m1(other, ctx).wait_recv()
        meta_sum = meta_sum + meta_ctx[other]
    meta[dp] = meta_sum
    z_own(mz)
    total = part[:, my_col].astype(F32)
    for other in reversed(others):
        p1(other, ctx).wait_recv()
        total = total + recv[other].astype(F32)
    emb[dp, :, my_col] = total.astype(BF16)
    z_own(zcopy)
    enter(0)
    from_a(3, 0)
    from_a(1, 0)
    from_b(0, 3, 0)
    z_near(zcopy)
    z_near(mz)
    enter(1)
    enter(2)
    from_b(0, 1, 0)
    from_a(2, 0)
    z_next(zcopy)
    z_next(mz)
    enter(3)
    enter(4)
    from_b(3, 3, 0)
    from_b(3, 1, 0)
    from_b(1, 3, 0)
    from_b(1, 1, 0)
    last(0, 0)
    from_a(1, 1)
    from_a(3, 1)
    from_b(0, 1, 1)
    from_a(1, 2)
    z_far(zcopy, (3, -3))
    enter(5)
    enter(6)
    from_b(0, 3, 1)
    from_a(3, 2)
    from_b(0, 1, 2)
    from_b(0, 3, 2)
    from_b(2, 1, 0)
    from_a(2, 1)
    from_b(2, 3, 0)
    from_a(1, 3)
    from_a(2, 2)
    from_a(3, 3)
    from_b(0, 1, 3)
    from_a(1, 4)
    from_b(0, 3, 3)
    from_a(3, 4)
    from_b(0, 1, 4)
    z_far(zcopy, (4,))
    enter(7)
    z_far(mz, (3, -3, 4))
    for k in range(1, NX):
        mx(x, mod(x + k, NX)).start()
    from_b(0, 3, 4)
    last(3, 0)
    from_a(2, 3)
    last(1, 0)
    from_b(1, 1, 1)
    from_a(2, 4)
    from_b(1, 3, 1)
    from_b(3, 1, 1)
    from_b(3, 3, 1)
    last(0, 1)
    from_b(1, 3, 2)
    from_b(1, 1, 2)
    from_a(3, 5)
    from_a(1, 5)
    from_b(0, 1, 5)
    from_a(1, 6)
    from_b(0, 3, 5)
    from_b(0, 1, 6)
    from_a(2, 5)
    from_a(3, 6)
    from_b(0, 3, 6)
    from_a(2, 6)
    from_b(3, 3, 2)
    from_b(3, 1, 2)
    last(0, 5)
    last(0, 2)
    last(2, 0)
    from_b(2, 3, 1)
    from_b(2, 1, 1)
    last(0, 6)
    from_b(1, 3, 3)
    from_b(1, 1, 3)
    from_b(2, 3, 2)
    from_b(2, 1, 2)
    from_b(3, 3, 3)
    from_b(3, 1, 3)
    last(0, 3)
    from_b(1, 3, 4)
    from_b(1, 1, 4)
    from_b(3, 3, 4)
    from_b(3, 1, 4)
    from_a(3, 7)
    from_a(1, 7)
    from_b(0, 1, 7)
    from_b(0, 3, 7)
    from_b(2, 1, 3)
    last(1, 1)
    from_b(2, 1, 4)
    from_a(2, 7)
    last(0, 4)
    from_b(3, 1, 5)
    from_b(2, 3, 3)
    from_b(2, 3, 4)
    last(0, 7)
    last(3, 1)
    from_b(1, 1, 5)
    last(1, 2)
    from_b(3, 3, 5)
    last(3, 5)
    from_b(1, 3, 5)
    from_b(1, 1, 6)
    from_b(1, 3, 6)
    from_b(2, 1, 5)
    from_b(3, 1, 6)
    last(1, 5)
    from_b(2, 1, 6)
    from_b(2, 3, 5)
    last(3, 2)
    last(1, 6)
    from_b(3, 3, 6)
    last(1, 3)
    last(2, 2)
    last(2, 6)
    last(3, 4)
    last(2, 5)
    from_b(2, 3, 6)
    from_b(3, 1, 7)
    last(2, 1)
    last(3, 3)
    last(3, 6)
    last(1, 4)
    from_b(1, 1, 7)
    from_b(3, 3, 7)
    from_b(1, 3, 7)
    last(3, 7)
    last(2, 4)
    from_b(2, 3, 7)
    from_b(2, 1, 7)
    last(1, 7)
    last(2, 3)
    last(2, 7)

    def gram_of(core, first_time):
        for yy in range(NY):
            col = pl.multiple_of((yy * 2 + core) * FB, FB)
            e = emb[:, :, pl.ds(col, FB)].reshape(ALL, FB)
            top = dot(e[0:HALF], e, ((1,), (1,)))
            low = dot(e[HALF:], e[HALF:], ((1,), (1,)))
            if first_time and yy == 0:
                gram[0:HALF, :] = top
                gram[HALF:, HALF:] = low
            else:
                gram[0:HALF, :] += top
                gram[HALF:, HALF:] += low

    gram_of(c, True)
    pltpu.make_async_remote_copy(
        src_ref=emb.at[pl.ds(0, N_DP // 2)], dst_ref=emb.at[pl.ds(0, N_DP // 2)],
        send_sem=s_send, recv_sem=s_recv, device_id=sibling, device_id_type=MESH,
    ).wait_recv()
    gram_of(1 - c, False)
    gram[HALF:, 0:HALF] = jnp.transpose(gram[0:HALF, HALF:])

    for k in range(1, NX):
        mx(mod(x + k, NX), x).wait_recv()

    inv_temp = it_ref[0]
    info = jnp.broadcast_to(meta[...], (N_DP, DOCS, 128)).reshape(ALL, 128)
    at = lax.broadcasted_iota(jnp.int32, (ALL, 128), 1) - mod(lax.broadcasted_iota(jnp.int32, (ALL, 128), 0), DOCS)
    pos_f = jnp.sum(jnp.where(at == 0, info, 0.0), axis=1, keepdims=True)
    pos_col = pos_f.astype(jnp.int32)
    count_col = jnp.sum(jnp.where(at == DOCS, info, 0.0), axis=1, keepdims=True)
    eye = lax.broadcasted_iota(jnp.int32, (RB, RB), 0) == lax.broadcasted_iota(jnp.int32, (RB, RB), 1)
    blocks = [slice(i * RB, (i + 1) * RB) for i in range(ALL // RB)]

    def as_row(cols):
        return jnp.concatenate(
            [jnp.sum(jnp.where(eye, jnp.broadcast_to(v, (RB, RB)), 0.0), axis=0, keepdims=True) for v in cols],
            axis=1,
        )

    q_cols = []
    for r in blocks:
        norm2 = jnp.sum(jnp.where(eye, gram[r, r], 0.0), axis=1, keepdims=True)
        inv_count = 1.0 / count_col[r]
        q_cols.append(inv_count * lax.rsqrt(norm2 * inv_count * inv_count + 1e-06))
    q_row = as_row(q_cols)
    pos_row = as_row([pos_f[r] for r in blocks]).astype(jnp.int32)

    lane_all = lax.broadcasted_iota(jnp.int32, (RB, ALL), 1)
    sub_all = lax.broadcasted_iota(jnp.int32, (RB, ALL), 0)
    lse_cols = []
    loss = jnp.zeros((1, 1), F32)
    for i, r in enumerate(blocks):
        logits = gram[r, :] * (q_cols[i] * inv_temp) * q_row
        parts = [logits[:, q] for q in blocks]
        parts[i] = jnp.where(eye, -1e30, parts[i])
        logits = jnp.concatenate(parts, axis=1)
        gram[r, :] = logits
        top = jnp.max(logits, axis=1, keepdims=True)
        sum_exp = jnp.sum(jnp.exp(logits - top), axis=1, keepdims=True)
        lse = top + jnp.log(sum_exp)
        at_pos = jnp.sum(jnp.where(lane_all == pos_col[r], logits, 0.0), axis=1, keepdims=True)
        loss = loss + jnp.sum(lse - at_pos, axis=0, keepdims=True)
        lse_cols.append(lse)
    loss_ref[...] = jnp.broadcast_to(loss * (1.0 / ALL), (1, 128))

    factor = inv_temp * (1.0 / ALL)
    shift_cols = [lse - jnp.log(jnp.broadcast_to(factor, (RB, 1))) for lse in lse_cols]
    shift_row = as_row(shift_cols)
    for i, r in enumerate(blocks):
        logits = gram[r, :]
        own = jnp.exp(logits - shift_cols[i])
        own = jnp.where(lane_all == pos_col[r], own - factor, own)
        other = jnp.exp(logits - shift_row)
        other = jnp.where(sub_all == pos_row - i * RB, other - factor, other)
        both = own.astype(BF16).astype(F32) + other.astype(BF16).astype(F32)
        along = jnp.sum(both * logits, axis=1, keepdims=True) * (1.0 / inv_temp)
        parts = [both[:, q] for q in blocks]
        parts[i] = jnp.where(eye, -along, parts[i])
        grads = jnp.concatenate(parts, axis=1) * q_cols[i] * q_row
        gram[r, :] = grads
        if i < 2:
            grads = jnp.concatenate([grads[:, 0:HALF], 2.0 * grads[:, HALF:]], axis=1)
        nmat[r, :] = grads.astype(BF16)

    n_own = gram[pl.ds(pl.multiple_of(dp * DOCS, DOCS), DOCS), :]
    n_hi = n_own.astype(BF16)
    n_own = jnp.concatenate([n_hi, (n_own - n_hi.astype(F32)).astype(BF16)], axis=0)
    n_top, n_low = nmat[0:HALF, :], nmat[HALF:, HALF:]
    for j in range(N_CTX):
        cols = slice(j * FB, (j + 1) * FB)
        e = emb[:, :, cols].reshape(ALL, FB)
        top = dot(n_top, e, ((1,), (0,))) * e[0:HALF].astype(F32)
        low = dot(n_low, e[HALF:], ((1,), (0,))) * e[HALF:].astype(F32)
        gain = gain_ref[:, cols]
        gg_ref[:, cols] = (jnp.sum(top, axis=0, keepdims=True) + jnp.sum(low, axis=0, keepdims=True)) / gain
        both = dot(n_own, e, ((1,), (0,)))
        g16 = (both[0:DOCS] + both[DOCS:]) * gain
        g_hi = g16.astype(BF16)
        gd_ref[0:DOCS, cols] = g_hi
        gd_ref[DOCS:, cols] = (g16 - g_hi.astype(F32)).astype(BF16)

    oh = jnp.concatenate([onehot, onehot, jnp.zeros((128 - 2 * DOCS, TOK), F32)], axis=0)
    oh_ref[...] = jnp.transpose(oh).astype(BF16)

    def sent(ref, sem):
        pltpu.make_async_remote_copy(
            src_ref=ref, dst_ref=ref, send_sem=sem, recv_sem=s_recv, device_id=sibling, device_id_type=MESH,
        ).wait_send()

    sent(recv.at[pl.ds(0, N_CTX - 1)], p1_send)
    sent(meta_ctx.at[pl.ds(0, N_CTX - 1)], m1_send)
    sent(emb.at[pl.ds(0, NZ - 1), :, pl.ds(0, FB)], z_send)
    sent(meta.at[pl.ds(0, NZ - 1)], mz_send)
    sent(meta.at[pl.ds(0, NZ * (NX - 1))], mx_send)
    sent(emb.at[pl.ds(0, 3)], a_send)
    sent(emb.at[pl.ds(0, 12)], b_send)
    sent(emb.at[pl.ds(0, 16)], s_send)


def final_kernel(h_ref, gd_ref, oh_ref, sc_ref, gg_ref, loss_ref, out_hbm, gg_out, loss_out, grad, out, sem):
    select = oh_ref[:, 0:2 * DOCS]
    acc = jnp.zeros((TOK, 128), F32)
    for j in range(D // FB):
        cols = slice(j * FB, (j + 1) * FB)
        rows = dot(select, gd_ref[:, cols], ((1,), (0,)))
        grad[:, cols] = rows
        rows = rows * h_ref[:, cols].astype(F32)
        for k in range(FB // 128):
            acc = acc + rows[:, k * 128:(k + 1) * 128]
    inner_all = jnp.sum(acc, axis=1, keepdims=True) * (1.0 / D)
    copies = []
    for i in range(TOK // ROWS):
        r = slice(i * ROWS, (i + 1) * ROWS)
        inner = inner_all[r]
        scale = sc_ref[r, 0:1]
        coef = scale * scale * scale * inner
        for j in range(D // 512):
            cols = slice(j * 512, (j + 1) * 512)
            out[r, cols] = (scale * grad[r, cols] - h_ref[r, cols].astype(F32) * coef).astype(BF16)
        copies.append(pltpu.make_async_copy(out.at[pl.ds(i * ROWS, ROWS)], out_hbm.at[0, pl.ds(i * ROWS, ROWS)], sem.at[i]))
        copies[-1].start()
    gg_out[...] = gg_ref[...]
    loss_out[...] = loss_ref[...]
    for copy in copies:
        copy.wait()


def body(hidden, segments, gain, inv_temp, positives):
    hbm = lambda v: pltpu.with_memory_space_constraint(v, pltpu.HBM)
    vmem = pl.BlockSpec(memory_space=pltpu.VMEM)
    in_hbm = pl.BlockSpec(memory_space=pltpu.HBM)
    smem = pl.BlockSpec(memory_space=pltpu.SMEM)
    dma = pltpu.SemaphoreType.DMA
    gd, oh, sc, gg, loss, h = pl.pallas_call(
        gather_kernel,
        name="pool_gather",
        out_shape=(
            jax.ShapeDtypeStruct((2 * DOCS, D), BF16),
            jax.ShapeDtypeStruct((TOK, 128), BF16),
            jax.ShapeDtypeStruct((TOK, 128), F32),
            jax.ShapeDtypeStruct((1, D), F32),
            jax.ShapeDtypeStruct((1, 128), F32),
            jax.ShapeDtypeStruct((TOK, D), BF16),
        ),
        in_specs=[in_hbm, in_hbm, smem, in_hbm, smem],
        out_specs=(vmem,) * 6,
        scratch_shapes=[
            pltpu.VMEM((1, TOK), jnp.int32),
            pltpu.VMEM((1, D), F32),
            pltpu.VMEM((DOCS, D), BF16),
            pltpu.VMEM((N_CTX, DOCS, FB), BF16),
            pltpu.VMEM((N_DP, DOCS, D), BF16),
            pltpu.VMEM((1, 128), F32),
            pltpu.VMEM((N_CTX, 1, 128), F32),
            pltpu.VMEM((N_DP, 1, 128), F32),
            pltpu.VMEM((ALL, ALL), F32),
            pltpu.VMEM((ALL, ALL), BF16),
            dma((2,)),
            dma((4,)),
            dma, dma((N_CTX,)), dma, dma((NZ,)), dma, dma((NX,)), dma, dma((N_CTX,)),
            dma, dma((NZ,)), dma, dma((24,)), dma, dma((96,)), dma, dma,
        ],
        compiler_params=pltpu.CompilerParams(collective_id=0, has_side_effects=True, vmem_limit_bytes=20 << 20),
    )(hbm(hidden[0]), hbm(segments), hbm(positives), hbm(gain.reshape(1, D)), inv_temp.reshape(1))

    grad_hidden, grad_gain, loss = pl.pallas_call(
        final_kernel,
        name="grad_hidden",
        out_shape=(
            jax.ShapeDtypeStruct((1, TOK, D), BF16),
            jax.ShapeDtypeStruct((1, D), F32),
            jax.ShapeDtypeStruct((1, 128), F32),
        ),
        in_specs=[vmem] * 6,
        out_specs=(pl.BlockSpec(memory_space=pltpu.HBM), vmem, vmem),
        scratch_shapes=[pltpu.VMEM((TOK, D), F32), pltpu.VMEM((TOK, D), BF16), dma((TOK // ROWS,))],
        compiler_params=pltpu.CompilerParams(vmem_limit_bytes=20 << 20),
    )(h, gd, oh, sc, gg, loss)
    return grad_hidden, grad_gain.reshape(D), loss[0, 0]


def solution(mesh):
    return jax.shard_map(
        body,
        mesh=mesh,
        in_specs=(P("dp", "ctx", None), P("dp", "ctx"), P(), P(), P(("dp", "ctx"))),
        out_specs=(P("dp", "ctx", None), P(), P()),
        check_vma=False,
    )
```

```python
import functools

import jax
import jax.numpy as jnp
from jax import lax
from jax.experimental import pallas as pl
from jax.experimental.pallas import tpu as pltpu
from jax.sharding import PartitionSpec as P

MESH = pl.DeviceIdType.MESH
F32 = jnp.float32
BF16 = jnp.bfloat16

NX, NY, NZ = 4, 4, 8
N_DP, N_CTX = NX * NZ, NY * 2
DOCS = 16
ALL = N_DP * DOCS
TOK = 256
D = 4096
FB = D // N_CTX
HALF = ALL // 2
ROWS = 32
DIRECT = (5, 6, 7)
RB = 128


def mod(a, n):
    return lax.rem(a, n)


def dot(a, b, dims):
    return lax.dot_general(a, b, (dims, ((), ())), preferred_element_type=F32)


def gather_kernel(
    h_hbm, seg_hbm, pos_ref, gain_hbm, it_ref,
    gd_ref, oh_ref, sc_ref, gg_ref, loss_ref, h,
    seg_ref, gain_ref, part, recv, emb, meta_own, meta_ctx, meta, gram, nmat,
    in_sem, h_sem, m1_send, m1_recv, mz_send, mz_recv, mx_send, mx_recv, p1_send, p1_recv,
    z_send, z_recv, a_send, a_recv, b_send, b_recv, s_send, s_recv,
):
    dp, ctx = lax.axis_index("dp"), lax.axis_index("ctx")
    x, z = lax.div(dp, NZ), mod(dp, NZ)
    y, c = lax.div(ctx, 2), mod(ctx, 2)
    a = (1 - c) * x + c * y
    b = (1 - c) * y + c * x

    seg_copy = pltpu.make_async_copy(seg_hbm, seg_ref, in_sem.at[0])
    seg_copy.start()
    h_copies = []
    for i in range(4):
        rows = pl.ds(i * (TOK // 4), TOK // 4)
        h_copies.append(pltpu.make_async_copy(h_hbm.at[rows], h.at[rows], h_sem.at[i]))
        h_copies[-1].start()
    gain_copy = pltpu.make_async_copy(gain_hbm, gain_ref, in_sem.at[1])
    gain_copy.start()

    def at_a(aa):
        return ((1 - c) * (aa * NZ + z) + c * dp, (1 - c) * ctx + c * (aa * 2 + c))

    def at_b(bb):
        return ((1 - c) * dp + c * (bb * NZ + z), (1 - c) * (bb * 2 + c) + c * ctx)

    sibling = (dp, ctx + 1 - 2 * c)

    barrier = pltpu.get_barrier_semaphore()
    peers = [(x * NZ + mod(z + k, NZ), ctx) for k in (2, 6, 1, 7)]
    peers += [(dp, mod(ctx + k, N_CTX)) for k in range(1, N_CTX)]
    peers += [(mod(x + k, NX) * NZ + z, ctx) for k in range(1, NX)]
    for peer in peers:
        pl.semaphore_signal(barrier, inc=1, device_id=peer, device_id_type=MESH)

    seg_copy.wait()
    seg = seg_ref[...]
    doc_rows = lax.broadcasted_iota(jnp.int32, (DOCS, TOK), 0)
    onehot = (seg == doc_rows).astype(F32)
    lane = lax.broadcasted_iota(jnp.int32, (DOCS, 128), 1)
    counts = jnp.where(
        lane == DOCS + lax.broadcasted_iota(jnp.int32, (DOCS, 128), 0), jnp.sum(onehot, axis=1, keepdims=True), 0.0
    )
    lane1 = lax.broadcasted_iota(jnp.int32, (1, 128), 1)
    pos = jnp.where(lane1 == 2 * ctx, pos_ref[0], jnp.where(lane1 == 2 * ctx + 1, pos_ref[1], 0))
    meta_own[...] = pos.astype(F32) + jnp.sum(counts, axis=0, keepdims=True)

    squares = []
    for i in range(4):
        h_copies[i].wait()
        acc = jnp.zeros((TOK // 4, 128), F32)
        for j in range(D // 128):
            v = h[i * (TOK // 4):(i + 1) * (TOK // 4), j * 128:(j + 1) * 128].astype(F32)
            acc = acc + v * v
        squares.append(jnp.sum(acc, axis=1, keepdims=True))
    mean_sq = jnp.concatenate(squares, axis=0) * (1.0 / D)
    scale = jnp.broadcast_to(lax.rsqrt(mean_sq + 1e-06), (TOK, 128))
    sc_ref[...] = scale
    weight = onehot * jnp.transpose(scale)[0:DOCS, :]
    w_hi = weight.astype(BF16)
    w_lo = (weight - w_hi.astype(F32)).astype(BF16)
    w2 = jnp.concatenate([w_hi, w_lo], axis=0)
    gain_copy.wait()

    def p1(src, dst):
        return pltpu.make_async_remote_copy(
            src_ref=part.at[:, pl.ds(pl.multiple_of(dst * FB, FB), FB)], dst_ref=recv.at[src],
            send_sem=p1_send, recv_sem=p1_recv.at[src], device_id=(dp, dst), device_id_type=MESH,
        )

    def m1(src, dst):
        return pltpu.make_async_remote_copy(
            src_ref=meta_own, dst_ref=meta_ctx.at[src],
            send_sem=m1_send, recv_sem=m1_recv.at[src], device_id=(dp, dst), device_id_type=MESH,
        )

    for j in range(N_CTX):
        cols = slice(j * FB, (j + 1) * FB)
        both = dot(w2, h[:, cols], ((1,), (0,)))
        part[:, cols] = ((both[0:DOCS] + both[DOCS:]) * gain_ref[:, cols]).astype(BF16)

    pl.semaphore_wait(barrier, len(peers))
    others = [mod(ctx + k, N_CTX) for k in (4, 5, 3, 2, 6, 7, 1)]
    for other in others:
        m1(ctx, other).start()
    for other in others:
        p1(ctx, other).start()

    my_col = pl.ds(pl.multiple_of(ctx * FB, FB), FB)

    def zcopy(zz, dst):
        ref = emb.at[x * NZ + zz, :, my_col]
        return pltpu.make_async_remote_copy(
            src_ref=ref, dst_ref=ref, send_sem=z_send, recv_sem=z_recv.at[zz],
            device_id=(x * NZ + dst, ctx), device_id_type=MESH,
        )

    def mz(zz, dst):
        ref = meta.at[x * NZ + zz]
        return pltpu.make_async_remote_copy(
            src_ref=ref, dst_ref=ref, send_sem=mz_send, recv_sem=mz_recv.at[zz],
            device_id=(x * NZ + dst, ctx), device_id_type=MESH,
        )

    def mx(xx, dst):
        ref = meta.at[pl.ds(xx * NZ, NZ)]
        return pltpu.make_async_remote_copy(
            src_ref=ref, dst_ref=ref, send_sem=mx_send, recv_sem=mx_recv.at[xx],
            device_id=(dst * NZ + z, ctx), device_id_type=MESH,
        )

    odd = mod(z, 2)
    z_off = lambda k: mod(z + k + NZ, NZ)
    first = [z, z_off(1), z_off(-1), z_off(2), z_off(-2), z_off(3), z_off(-3), z_off(4)]
    size = [1] * NZ

    def z_own(copy):
        for k in (1, -1, 2, -2):
            copy(z, z_off(k)).start()

    def z_near(copy):
        for k in (1, -1):
            copy(z_off(k), z).wait_recv()
            copy(z_off(k), z_off(-2 * k)).start()

    def z_next(copy):
        way = 2 - 4 * odd
        for k in (2, -2):
            copy(z_off(k), z).wait_recv()
        copy(z_off(way), z_off(-way)).start()

    def z_far(copy, ks):
        for k in ks:
            copy(z_off(k), z).wait_recv()

    a_off = lambda k: mod(a + k, NX)
    b_off = lambda k: mod(b + k, NX)

    def block(aa, bb, g):
        xx = (1 - c) * aa + c * bb
        yy = (1 - c) * bb + c * aa
        col = pl.multiple_of((yy * 2 + c) * FB, FB)
        return emb.at[pl.ds(xx * NZ + first[g], size[g]), :, pl.ds(col, FB)]

    def acopy(am, g, way, to):
        ref = block(a_off(am), b, g)
        return pltpu.make_async_remote_copy(
            src_ref=ref, dst_ref=ref, send_sem=a_send, recv_sem=a_recv.at[3 * g + way],
            device_id=at_a(to), device_id_type=MESH,
        )

    def bcopy(am, bm, g, way, to):
        ref = block(a_off(am), b_off(bm), g)
        return pltpu.make_async_remote_copy(
            src_ref=ref, dst_ref=ref, send_sem=b_send, recv_sem=b_recv.at[12 * g + 3 * am + way],
            device_id=at_b(to), device_id_type=MESH,
        )

    def sib(am, bm, g):
        ref = block(a_off(am), b_off(bm), g)
        pltpu.make_async_remote_copy(
            src_ref=ref, dst_ref=ref, send_sem=s_send, recv_sem=s_recv,
            device_id=sibling, device_id_type=MESH,
        ).start()

    def spread(am, g):
        bcopy(am, 0, g, 0, b_off(1)).start()
        bcopy(am, 0, g, 1, b_off(3)).start()
        if g in DIRECT:
            bcopy(am, 0, g, 2, b_off(2)).start()
        sib(am, 0, g)

    def enter(g):
        for way, k in ((0, 1), (1, 3), (2, 2)):
            acopy(0, g, way, a_off(k)).start()
        spread(0, g)

    def from_a(am, g):
        acopy(am, g, {3: 0, 1: 1, 2: 2}[am], a).wait_recv()
        spread(am, g)

    def from_b(am, bm, g):
        bcopy(am, bm, g, 0 if bm == 3 else 1, b).wait_recv()
        if g not in DIRECT and bm == (3 if (g + (am >= 2)) % 2 == 0 else 1):
            bcopy(am, bm, g, 2, b_off(4 - bm)).start()
        sib(am, bm, g)

    def last(am, g):
        bcopy(am, 2, g, 2, b).wait_recv()
        sib(am, 2, g)

    meta_sum = meta_own[...]
    for other in reversed(others):
        m1(other, ctx).wait_recv()
        meta_sum = meta_sum + meta_ctx[other]
    meta[dp] = meta_sum
    z_own(mz)
    total = part[:, my_col].astype(F32)
    for other in reversed(others):
        p1(other, ctx).wait_recv()
        total = total + recv[other].astype(F32)
    emb[dp, :, my_col] = total.astype(BF16)
    z_own(zcopy)
    enter(0)
    from_a(3, 0)
    from_a(1, 0)
    from_b(0, 3, 0)
    z_near(zcopy)
    z_near(mz)
    enter(1)
    enter(2)
    from_b(0, 1, 0)
    from_a(2, 0)
    z_next(zcopy)
    z_next(mz)
    enter(3)
    enter(4)
    from_b(3, 3, 0)
    from_b(3, 1, 0)
    from_b(1, 3, 0)
    from_b(1, 1, 0)
    last(0, 0)
    from_a(1, 1)
    from_a(3, 1)
    from_b(0, 1, 1)
    from_a(1, 2)
    z_far(zcopy, (3, -3))
    enter(5)
    enter(6)
    from_b(0, 3, 1)
    from_a(3, 2)
    from_b(0, 1, 2)
    from_b(0, 3, 2)
    from_b(2, 1, 0)
    from_a(2, 1)
    from_b(2, 3, 0)
    from_a(1, 3)
    from_a(2, 2)
    from_a(3, 3)
    from_b(0, 1, 3)
    from_a(1, 4)
    from_b(0, 3, 3)
    from_a(3, 4)
    from_b(0, 1, 4)
    z_far(zcopy, (4,))
    enter(7)
    z_far(mz, (3, -3, 4))
    for k in range(1, NX):
        mx(x, mod(x + k, NX)).start()
    from_b(0, 3, 4)
    last(3, 0)
    from_a(2, 3)
    last(1, 0)
    from_b(1, 1, 1)
    from_a(2, 4)
    from_b(1, 3, 1)
    from_b(3, 1, 1)
    from_b(3, 3, 1)
    last(0, 1)
    from_b(1, 3, 2)
    from_b(1, 1, 2)
    from_a(3, 5)
    from_a(1, 5)
    from_b(0, 1, 5)
    from_a(1, 6)
    from_b(0, 3, 5)
    from_b(0, 1, 6)
    from_a(2, 5)
    from_a(3, 6)
    from_b(0, 3, 6)
    from_a(2, 6)
    from_b(3, 3, 2)
    from_b(3, 1, 2)
    last(0, 5)
    last(0, 2)
    last(2, 0)
    from_b(2, 3, 1)
    from_b(2, 1, 1)
    last(0, 6)
    from_b(1, 3, 3)
    from_b(1, 1, 3)
    from_b(2, 3, 2)
    from_b(2, 1, 2)
    from_b(3, 3, 3)
    from_b(3, 1, 3)
    last(0, 3)
    from_b(1, 3, 4)
    from_b(1, 1, 4)
    from_b(3, 3, 4)
    from_b(3, 1, 4)
    from_a(3, 7)
    from_a(1, 7)
    from_b(0, 1, 7)
    from_b(0, 3, 7)
    from_b(2, 1, 3)
    last(1, 1)
    from_b(2, 1, 4)
    from_a(2, 7)
    last(0, 4)
    from_b(3, 1, 5)
    from_b(2, 3, 3)
    from_b(2, 3, 4)
    last(0, 7)
    last(3, 1)
    from_b(1, 1, 5)
    last(1, 2)
    from_b(3, 3, 5)
    last(3, 5)
    from_b(1, 3, 5)
    from_b(1, 1, 6)
    from_b(1, 3, 6)
    from_b(2, 1, 5)
    from_b(3, 1, 6)
    last(1, 5)
    from_b(2, 1, 6)
    from_b(2, 3, 5)
    last(3, 2)
    last(1, 6)
    from_b(3, 3, 6)
    last(1, 3)
    last(2, 2)
    last(2, 6)
    last(3, 4)
    last(2, 5)
    from_b(2, 3, 6)
    from_b(3, 1, 7)
    last(2, 1)
    last(3, 3)
    last(3, 6)
    last(1, 4)
    from_b(1, 1, 7)
    from_b(3, 3, 7)
    from_b(1, 3, 7)
    last(3, 7)
    last(2, 4)
    from_b(2, 3, 7)
    from_b(2, 1, 7)
    last(1, 7)
    last(2, 3)
    last(2, 7)

    def gram_of(core, first_time):
        for yy in range(NY):
            col = pl.multiple_of((yy * 2 + core) * FB, FB)
            e = emb[:, :, pl.ds(col, FB)].reshape(ALL, FB)
            top = dot(e[0:HALF], e, ((1,), (1,)))
            low = dot(e[HALF:], e[HALF:], ((1,), (1,)))
            if first_time and yy == 0:
                gram[0:HALF, :] = top
                gram[HALF:, HALF:] = low
            else:
                gram[0:HALF, :] += top
                gram[HALF:, HALF:] += low

    gram_of(c, True)
    pltpu.make_async_remote_copy(
        src_ref=emb.at[pl.ds(0, N_DP // 2)], dst_ref=emb.at[pl.ds(0, N_DP // 2)],
        send_sem=s_send, recv_sem=s_recv, device_id=sibling, device_id_type=MESH,
    ).wait_recv()
    for k in range(1, NX):
        mx(mod(x + k, NX), x).wait_recv()
    inv_temp = it_ref[0]
    info = jnp.broadcast_to(meta[...], (N_DP, DOCS, 128)).reshape(ALL, 128)
    at = lax.broadcasted_iota(jnp.int32, (ALL, 128), 1) - mod(lax.broadcasted_iota(jnp.int32, (ALL, 128), 0), DOCS)
    pos_f = jnp.sum(jnp.where(at == 0, info, 0.0), axis=1, keepdims=True)
    pos_col = pos_f.astype(jnp.int32)
    count_col = jnp.sum(jnp.where(at == DOCS, info, 0.0), axis=1, keepdims=True)
    eye = lax.broadcasted_iota(jnp.int32, (RB, RB), 0) == lax.broadcasted_iota(jnp.int32, (RB, RB), 1)
    blocks = [slice(i * RB, (i + 1) * RB) for i in range(ALL // RB)]

    def as_row(cols):
        return jnp.concatenate(
            [jnp.sum(jnp.where(eye, jnp.broadcast_to(v, (RB, RB)), 0.0), axis=0, keepdims=True) for v in cols],
            axis=1,
        )
    pos_row = as_row([pos_f[r] for r in blocks]).astype(jnp.int32)

    gram_of(1 - c, False)
    gram[HALF:, 0:HALF] = jnp.transpose(gram[0:HALF, HALF:])


    q_cols = []
    for r in blocks:
        norm2 = jnp.sum(jnp.where(eye, gram[r, r], 0.0), axis=1, keepdims=True)
        inv_count = 1.0 / count_col[r]
        q_cols.append(inv_count * lax.rsqrt(norm2 * inv_count * inv_count + 1e-06))
    q_row = as_row(q_cols)

    lane_all = lax.broadcasted_iota(jnp.int32, (RB, ALL), 1)
    sub_all = lax.broadcasted_iota(jnp.int32, (RB, ALL), 0)
    lse_cols = []
    loss = jnp.zeros((1, 1), F32)
    for i, r in enumerate(blocks):
        logits = gram[r, :] * (q_cols[i] * inv_temp) * q_row
        parts = [logits[:, q] for q in blocks]
        parts[i] = jnp.where(eye, -1e30, parts[i])
        logits = jnp.concatenate(parts, axis=1)
        gram[r, :] = logits
        top = jnp.max(logits, axis=1, keepdims=True)
        sum_exp = jnp.sum(jnp.exp(logits - top), axis=1, keepdims=True)
        lse = top + jnp.log(sum_exp)
        at_pos = jnp.sum(jnp.where(lane_all == pos_col[r], logits, 0.0), axis=1, keepdims=True)
        loss = loss + jnp.sum(lse - at_pos, axis=0, keepdims=True)
        lse_cols.append(lse)
    loss_ref[...] = jnp.broadcast_to(loss * (1.0 / ALL), (1, 128))

    factor = inv_temp * (1.0 / ALL)
    shift_cols = [lse - jnp.log(jnp.broadcast_to(factor, (RB, 1))) for lse in lse_cols]
    shift_row = as_row(shift_cols)
    for i, r in enumerate(blocks):
        logits = gram[r, :]
        own = jnp.exp(logits - shift_cols[i])
        own = jnp.where(lane_all == pos_col[r], own - factor, own)
        other = jnp.exp(logits - shift_row)
        other = jnp.where(sub_all == pos_row - i * RB, other - factor, other)
        both = own.astype(BF16).astype(F32) + other.astype(BF16).astype(F32)
        along = jnp.sum(both * logits, axis=1, keepdims=True) * (1.0 / inv_temp)
        parts = [both[:, q] for q in blocks]
        parts[i] = jnp.where(eye, -along, parts[i])
        grads = jnp.concatenate(parts, axis=1) * q_cols[i] * q_row
        gram[r, :] = grads
        if i < 2:
            grads = jnp.concatenate([grads[:, 0:HALF], 2.0 * grads[:, HALF:]], axis=1)
        nmat[r, :] = grads.astype(BF16)

    n_own = gram[pl.ds(pl.multiple_of(dp * DOCS, DOCS), DOCS), :]
    n_hi = n_own.astype(BF16)
    n_own = jnp.concatenate([n_hi, (n_own - n_hi.astype(F32)).astype(BF16)], axis=0)
    n_top, n_low = nmat[0:HALF, :], nmat[HALF:, HALF:]
    for j in range(N_CTX):
        cols = slice(j * FB, (j + 1) * FB)
        e = emb[:, :, cols].reshape(ALL, FB)
        top = dot(n_top, e, ((1,), (0,))) * e[0:HALF].astype(F32)
        low = dot(n_low, e[HALF:], ((1,), (0,))) * e[HALF:].astype(F32)
        gain = gain_ref[:, cols]
        gg_ref[:, cols] = (jnp.sum(top, axis=0, keepdims=True) + jnp.sum(low, axis=0, keepdims=True)) / gain
        both = dot(n_own, e, ((1,), (0,)))
        g16 = (both[0:DOCS] + both[DOCS:]) * gain
        g_hi = g16.astype(BF16)
        gd_ref[0:DOCS, cols] = g_hi
        gd_ref[DOCS:, cols] = (g16 - g_hi.astype(F32)).astype(BF16)

    oh = jnp.concatenate([onehot, onehot, jnp.zeros((128 - 2 * DOCS, TOK), F32)], axis=0)
    oh_ref[...] = jnp.transpose(oh).astype(BF16)

    def sent(ref, sem):
        pltpu.make_async_remote_copy(
            src_ref=ref, dst_ref=ref, send_sem=sem, recv_sem=s_recv, device_id=sibling, device_id_type=MESH,
        ).wait_send()

    sent(recv.at[pl.ds(0, N_CTX - 1)], p1_send)
    sent(meta_ctx.at[pl.ds(0, N_CTX - 1)], m1_send)
    sent(emb.at[pl.ds(0, NZ - 1), :, pl.ds(0, FB)], z_send)
    sent(meta.at[pl.ds(0, NZ - 1)], mz_send)
    sent(meta.at[pl.ds(0, NZ * (NX - 1))], mx_send)
    sent(emb.at[pl.ds(0, 3)], a_send)
    sent(emb.at[pl.ds(0, 12)], b_send)
    sent(emb.at[pl.ds(0, 16)], s_send)


def final_kernel(h_ref, gd_ref, oh_ref, sc_ref, gg_ref, loss_ref, out_hbm, gg_out, loss_out, grad, out, sem):
    select = oh_ref[:, 0:2 * DOCS]
    acc = jnp.zeros((TOK, 128), F32)
    for j in range(D // FB):
        cols = slice(j * FB, (j + 1) * FB)
        rows = dot(select, gd_ref[:, cols], ((1,), (0,)))
        grad[:, cols] = rows
        rows = rows * h_ref[:, cols].astype(F32)
        for k in range(FB // 128):
            acc = acc + rows[:, k * 128:(k + 1) * 128]
    inner_all = jnp.sum(acc, axis=1, keepdims=True) * (1.0 / D)
    copies = []
    for i in range(TOK // ROWS):
        r = slice(i * ROWS, (i + 1) * ROWS)
        inner = inner_all[r]
        scale = sc_ref[r, 0:1]
        coef = scale * scale * scale * inner
        for j in range(D // 512):
            cols = slice(j * 512, (j + 1) * 512)
            out[r, cols] = (scale * grad[r, cols] - h_ref[r, cols].astype(F32) * coef).astype(BF16)
        copies.append(pltpu.make_async_copy(out.at[pl.ds(i * ROWS, ROWS)], out_hbm.at[0, pl.ds(i * ROWS, ROWS)], sem.at[i]))
        copies[-1].start()
    gg_out[...] = gg_ref[...]
    loss_out[...] = loss_ref[...]
    for copy in copies:
        copy.wait()


def body(hidden, segments, gain, inv_temp, positives):
    hbm = lambda v: pltpu.with_memory_space_constraint(v, pltpu.HBM)
    vmem = pl.BlockSpec(memory_space=pltpu.VMEM)
    in_hbm = pl.BlockSpec(memory_space=pltpu.HBM)
    smem = pl.BlockSpec(memory_space=pltpu.SMEM)
    dma = pltpu.SemaphoreType.DMA
    gd, oh, sc, gg, loss, h = pl.pallas_call(
        gather_kernel,
        name="pool_gather",
        out_shape=(
            jax.ShapeDtypeStruct((2 * DOCS, D), BF16),
            jax.ShapeDtypeStruct((TOK, 128), BF16),
            jax.ShapeDtypeStruct((TOK, 128), F32),
            jax.ShapeDtypeStruct((1, D), F32),
            jax.ShapeDtypeStruct((1, 128), F32),
            jax.ShapeDtypeStruct((TOK, D), BF16),
        ),
        in_specs=[in_hbm, in_hbm, smem, in_hbm, smem],
        out_specs=(vmem,) * 6,
        scratch_shapes=[
            pltpu.VMEM((1, TOK), jnp.int32),
            pltpu.VMEM((1, D), F32),
            pltpu.VMEM((DOCS, D), BF16),
            pltpu.VMEM((N_CTX, DOCS, FB), BF16),
            pltpu.VMEM((N_DP, DOCS, D), BF16),
            pltpu.VMEM((1, 128), F32),
            pltpu.VMEM((N_CTX, 1, 128), F32),
            pltpu.VMEM((N_DP, 1, 128), F32),
            pltpu.VMEM((ALL, ALL), F32),
            pltpu.VMEM((ALL, ALL), BF16),
            dma((2,)),
            dma((4,)),
            dma, dma((N_CTX,)), dma, dma((NZ,)), dma, dma((NX,)), dma, dma((N_CTX,)),
            dma, dma((NZ,)), dma, dma((24,)), dma, dma((96,)), dma, dma,
        ],
        compiler_params=pltpu.CompilerParams(collective_id=0, has_side_effects=True, vmem_limit_bytes=20 << 20),
    )(hbm(hidden[0]), hbm(segments), hbm(positives), hbm(gain.reshape(1, D)), inv_temp.reshape(1))

    grad_hidden, grad_gain, loss = pl.pallas_call(
        final_kernel,
        name="grad_hidden",
        out_shape=(
            jax.ShapeDtypeStruct((1, TOK, D), BF16),
            jax.ShapeDtypeStruct((1, D), F32),
            jax.ShapeDtypeStruct((1, 128), F32),
        ),
        in_specs=[vmem] * 6,
        out_specs=(pl.BlockSpec(memory_space=pltpu.HBM), vmem, vmem),
        scratch_shapes=[pltpu.VMEM((TOK, D), F32), pltpu.VMEM((TOK, D), BF16), dma((TOK // ROWS,))],
        compiler_params=pltpu.CompilerParams(vmem_limit_bytes=20 << 20),
    )(h, gd, oh, sc, gg, loss)
    return grad_hidden, grad_gain.reshape(D), loss[0, 0]


def solution(mesh):
    return jax.shard_map(
        body,
        mesh=mesh,
        in_specs=(P("dp", "ctx", None), P("dp", "ctx"), P(), P(), P(("dp", "ctx"))),
        out_specs=(P("dp", "ctx", None), P(), P()),
        check_vma=False,
    )
```
